32 devices in a mesh: bag: 4 (over y, x), seq: 8 (over z, core).
Axes of the slice: x: 2, y: 2, z: 4, core: 2. Of those that a mesh axis runs over, the one named last changes fastest.
Arguments:
- text_rows: bfloat16 [2048, 3072], P(('bag', 'seq')), may hold values from -6 to 6
- image_rows: bfloat16 [1024, 3072], P(('bag', 'seq')), may hold values from -6 to 6
- modulation: float32 [32, 2, 2, 3072], P('bag'), may hold values from -3 to 3
- head_weight: bfloat16 [2, 3072, 6144], P(None, None, 'seq'), may hold values from -0.109375 to 0.109375
- norm_gain: float32 [2, 2, 128], replicated, may hold values from 0.5 to 20
- store_down: bfloat16 [128, 2, 64, 3072], P('bag', None, 'seq'), may hold values from -0.109375 to 0.109375
- store_up: bfloat16 [128, 2, 64, 6144], P('bag', None, None, 'seq'), may hold values from -0.375 to 0.375
- store_row: int32 [128], replicated, may hold values from 0 to 127, as said below
- user_adapter: int32 [4, 4], replicated, may hold values from 0 to 127, as said below
- image_lengths: int32 [4, 4], P('bag'), may hold values from 1 to 64, 128 in all within a row
Outputs:
- text_out: bfloat16 [2048, 2048], P(('bag', 'seq'))
- image_out: bfloat16 [1024, 2048], P(('bag', 'seq'))
The draws below stay inside these ranges and needn't reach their ends.
Inputs may be any that keep to these rules, and one draw needn't show every extreme that they name: A permutation: adapter a is kept at row store_row[a] of store_down and store_up, whose owner is store_row[a] // 32. `user_adapter`: the 4 users of one bag have adapters kept by 4 different owners, so every owner keeps exactly one adapter of each bag.
All inputs are finite; a program needn't handle non-finite values.
Results may differ from the reference program's by a relative error of at most 0.04.
The reference program's roundings to bfloat16 on the way count: a program that leaves them out, or rounds other values in their place, can miss the bound.
Values may be sent and summed in bfloat16 or wider, within the bound.
No kernel may reach another device: no remote copies, remote signals or barrier semaphores. Data moves between devices by JAX's collectives and lax.ppermute only.
A program may use at most 128 MiB of HBM per device.

```python
import math
import jax
import jax.numpy as jnp
import numpy as np
from jax import lax

D = 3072
HEAD_DIM = 128
HEADS = 16
RANK = 64
TEXT = 64
ADAPT_DEV = 32
USERS = 4
SEGMENTS = 8
TEXT_BAG = 512
IMAGE_BAG = 256
ROWS_BAG = 768
ADAPTERS = 128
N_BAG = 4


def adapter_layout(key):
    base_key = jax.random.fold_in(key, 11)
    perm_key, owner_key, slot_key = jax.random.split(base_key, 3)
    placement = jax.random.permutation(perm_key, ADAPTERS).astype(jnp.int32)
    inverse = jnp.argsort(placement).astype(jnp.int32)
    owner_keys = jax.random.split(owner_key, N_BAG)
    owner_lists = jax.vmap(lambda one_key: jax.random.permutation(one_key, N_BAG))(owner_keys)[:, :USERS].astype(jnp.int32)
    slot_pick = jax.random.randint(slot_key, (N_BAG, USERS), 0, ADAPT_DEV).astype(jnp.int32)
    store_rows = owner_lists * ADAPT_DEV + slot_pick
    return (placement, jnp.take(inverse, store_rows, axis=0).astype(jnp.int32))


def draw_store_row(key, part):
    return adapter_layout(key)[0]


def draw_user_adapter(key, part):
    return adapter_layout(key)[1]


def draw_norm_gain(key, part):
    value_key = jax.random.fold_in(jax.random.fold_in(key, 5), 0)
    return jnp.exp(jax.random.uniform(value_key, (2, 2, HEAD_DIM), jnp.float32, math.log(0.6), math.log(1.6))).astype(jnp.float32)


def block_levels(rng, dims, shards, least, high):
    gain, own = 1.0, jax.random.fold_in(rng, 6)
    for axis_at, blocks in shards:
        draws = jnp.exp(jax.random.uniform(jax.random.fold_in(own, axis_at), (blocks,), jnp.float32, least / len(shards), high / len(shards)))
        gain = gain * jnp.repeat(draws, dims[axis_at] // blocks).reshape([-1 if axis == axis_at else 1 for axis in range(len(dims))])
    return gain


def profile(number_of, total, reach, slope):
    portions = [(1 << 20) // math.isqrt(standing ** slope) + 1 for standing in range(2, number_of + 1)]
    spare, holding = total - reach - (number_of - 1), [1] * (number_of - 1)
    while spare > 0:
        free = [i for i in range(number_of - 1) if holding[i] < reach]
        whole, left = sum([portions[i] for i in free]), spare
        for i in free:
            more = min(reach - holding[i], max(1, left * portions[i] // whole), spare)
            holding[i] = holding[i] + more
            spare = spare - more
    return np.array([reach] + holding)


def uneven_parts(stream_key, number_of, total, bound, skew):
    if number_of == 2:
        one = jax.random.randint(stream_key, (), max(1, total - bound), min(bound, total - 1) + 1)
        return jnp.stack([one, total - one])
    tallies = jnp.asarray(profile(number_of, total, bound, skew), jnp.int32)
    couples = (number_of - 1) // 2
    donor, receiver = tallies[1:1 + 2 * couples:2], tallies[2:2 + 2 * couples:2]
    margin = jnp.minimum(donor - 1, bound - receiver)
    moved = jax.random.randint(jax.random.fold_in(stream_key, 1), (couples,), 0, 1 << 20) % (margin + 1)
    tallies = tallies.at[1:1 + 2 * couples:2].set(donor - moved).at[2:2 + 2 * couples:2].set(receiver + moved)
    return tallies[jax.random.permutation(jax.random.fold_in(stream_key, 2), number_of)]


def normal_values(key, shape, width, limit, shards=(), kind=jnp.bfloat16):
    gain = block_levels(key, shape, shards, -0.22, 0.18) if shards else 1.0
    entries = jax.random.normal(key, shape, jnp.float32) * width * gain
    return jnp.minimum(jnp.maximum(entries, -limit), limit).astype(kind)


def setup_inputs(seed: int = 0) -> dict:
    key_of = jax.random.split(jax.random.key(seed), 11)
    text_rows = normal_values(key_of[0], (N_BAG * TEXT_BAG, D), 1.0, 6.0, ((0, 32),))
    image_rows = normal_values(key_of[1], (N_BAG * IMAGE_BAG, D), 1.0, 6.0, ((0, 32),))
    modulation = normal_values(key_of[2], (N_BAG * SEGMENTS, 2, 2, D), 0.5, 3.0, ((0, 4),), jnp.float32)
    head_weight = normal_values(key_of[3], (2, D, 3 * HEADS * HEAD_DIM), D ** -0.5, 0.109375, ((2, 8),))
    norm_gain = draw_norm_gain(jax.random.fold_in(key_of[10], 71), 0)
    store_down = normal_values(key_of[5], (ADAPTERS, 2, RANK, D), D ** -0.5, 0.109375, ((0, 4), (2, 8)))
    store_up = normal_values(key_of[6], (ADAPTERS, 2, RANK, 3 * HEADS * HEAD_DIM), (4 * RANK) ** -0.5, 0.375, ((0, 4), (3, 8)))
    store_row = draw_store_row(jax.random.fold_in(key_of[10], 71), 0)
    user_adapter = draw_user_adapter(jax.random.fold_in(key_of[10], 71), 0)
    image_lengths = jax.vmap(lambda own: uneven_parts(own, USERS, IMAGE_BAG // 2, IMAGE_BAG // 4, 2))(jax.random.split(key_of[9], N_BAG)).reshape((N_BAG, USERS)).astype(jnp.int32)
    return {"text_rows": text_rows, "image_rows": image_rows, "modulation": modulation, "head_weight": head_weight, "norm_gain": norm_gain, "store_down": store_down, "store_up": store_up, "store_row": store_row, "user_adapter": user_adapter, "image_lengths": image_lengths}


def modulate(raw_rows, shifts, scales):
    values = raw_rows.astype(jnp.float32)
    centre = values - lax.optimization_barrier(jnp.mean(values, axis=-1, keepdims=True))
    spread = lax.optimization_barrier(jnp.mean(centre * centre, axis=-1, keepdims=True))
    normed = centre * lax.rsqrt(spread + 1e-06)
    return ((1.0 + scales) * normed + shifts).astype(jnp.bfloat16)

def head_normed(values, gain_row):
    spread = lax.optimization_barrier(jnp.mean(values * values, axis=-1, keepdims=True))
    return (values * lax.rsqrt(spread + 1e-06) * gain_row).astype(jnp.bfloat16)

def attend(queries, keys_all, values_all, seg_ids):
    row_total = queries.shape[0]
    block_rows = math.gcd(row_total, 1024)
    query_blocks = queries.reshape(row_total // block_rows, block_rows, queries.shape[1])
    seg_blocks = seg_ids.reshape(row_total // block_rows, block_rows)
    factor = 1.0 / math.sqrt(queries.shape[1])

    def one_block(block_pair):
        query_rows, query_segs = block_pair
        scores = jnp.dot(query_rows, keys_all.T, preferred_element_type=jnp.float32) * factor
        scores = jnp.where(query_segs[:, None] == seg_ids[None, :], scores, -1e+30)
        top_score = lax.optimization_barrier(jnp.max(scores, axis=1, keepdims=True))
        weights = jnp.exp(scores - top_score)
        prob_rows = (weights / lax.optimization_barrier(jnp.sum(weights, axis=1, keepdims=True))).astype(jnp.bfloat16)
        return jnp.dot(prob_rows, values_all, preferred_element_type=jnp.float32).astype(jnp.bfloat16)
    return lax.map(one_block, (query_blocks, seg_blocks)).reshape(row_total, values_all.shape[1])

def adapted(hidden, weight, down_users, up_users, user_ids, gain_pair):
    row_count = hidden.shape[0]
    user_count = down_users.shape[0]
    user_pick = user_ids[:, None] == jnp.arange(user_count, dtype=jnp.int32)[None, :]
    plain_part = jnp.dot(hidden, weight, preferred_element_type=jnp.float32)
    all_users = jnp.einsum('nd,urd->nur', hidden.astype(jnp.float32), down_users.astype(jnp.float32))
    ranks = lax.optimization_barrier(jnp.sum(all_users * user_pick.astype(jnp.float32)[:, :, None], axis=1)).astype(jnp.bfloat16)
    spread_ranks = (user_pick.astype(jnp.bfloat16)[:, :, None] * ranks[:, None, :]).reshape(row_count, -1)
    adjust = jnp.dot(spread_ranks, up_users.reshape(-1, weight.shape[1]), preferred_element_type=jnp.float32)
    mixed_cols = (plain_part + adjust).reshape(row_count, HEADS, 3, HEAD_DIM)
    query = head_normed(mixed_cols[:, :, 0], gain_pair[0])
    key_rows = head_normed(mixed_cols[:, :, 1], gain_pair[1])
    value_rows = mixed_cols[:, :, 2].astype(jnp.bfloat16)
    return (query, key_rows, value_rows)

def reference(text_rows, image_rows, modulation, head_weight, norm_gain, store_down, store_up, store_row, user_adapter, image_lengths):
    text_bags = text_rows.reshape(N_BAG, TEXT_BAG, D)
    image_bags = image_rows.reshape(N_BAG, IMAGE_BAG, D)
    mod_bags = modulation.reshape(N_BAG, SEGMENTS, 2, 2, D)
    text_segs = jnp.arange(TEXT_BAG, dtype=jnp.int32) // TEXT

    def one_bag(bag_items):
        text_bag, image_bag, mod_bag, adapters, lengths = bag_items
        seg_ends = jnp.cumsum(jnp.repeat(lengths, 2))
        image_segs = lax.optimization_barrier(jnp.sum((jnp.arange(IMAGE_BAG, dtype=jnp.int32)[:, None] >= seg_ends[None, :]).astype(jnp.int32), axis=1)).astype(jnp.int32)
        chosen = jnp.take(store_row, adapters, axis=0)
        down_sel = jnp.take(store_down, chosen, axis=0)
        up_sel = jnp.take(store_up, chosen, axis=0)
        text_hidden = modulate(text_bag, mod_bag[text_segs, 0, 0], mod_bag[text_segs, 0, 1])
        image_hidden = modulate(image_bag, mod_bag[image_segs, 1, 0], mod_bag[image_segs, 1, 1])
        text_parts = adapted(text_hidden, head_weight[0], down_sel[:, 0], up_sel[:, 0], text_segs // 2, norm_gain[0])
        image_parts = adapted(image_hidden, head_weight[1], down_sel[:, 1], up_sel[:, 1], image_segs // 2, norm_gain[1])
        joined = [jnp.transpose(jnp.concatenate([text_parts[which], image_parts[which]], axis=0), (1, 0, 2)) for which in range(3)]
        seg_all = jnp.concatenate([text_segs, image_segs], axis=0)

        def one_head(head_rows):
            return attend(head_rows[0], head_rows[1], head_rows[2], seg_all)
        outputs = lax.map(one_head, (joined[0], joined[1], joined[2]))
        outputs = jnp.transpose(outputs, (1, 0, 2)).reshape(ROWS_BAG, HEADS * HEAD_DIM)
        return (outputs[:TEXT_BAG], outputs[TEXT_BAG:])
    text_out, image_out = lax.map(one_bag, (text_bags, image_bags, mod_bags, user_adapter, image_lengths))
    return (text_out.reshape(N_BAG * TEXT_BAG, HEADS * HEAD_DIM), image_out.reshape(N_BAG * IMAGE_BAG, HEADS * HEAD_DIM))
```

```python
import functools
import math

import jax
import jax.numpy as jnp
from jax import lax
from jax.experimental import pallas as pl
from jax.experimental.pallas import tpu as pltpu
from jax.sharding import PartitionSpec as P


HEAD_DIM = 128
TEXT = 64
CORES = 2
ROW_STEP = 16


VMEM_GRANT = 26 << 20
PARAMS = pltpu.CompilerParams(vmem_limit_bytes=VMEM_GRANT)

SMEM = functools.partial(pl.BlockSpec, memory_space=pltpu.SMEM)
VMEM = functools.partial(pl.BlockSpec, memory_space=pltpu.VMEM)
HBM = functools.partial(pl.BlockSpec, memory_space=pltpu.HBM)
NT = (((1,), (1,)), ((), ()))
TN = (((0,), (0,)), ((), ()))


def round_up(value, step):
    return -(-value // step) * step


class Plan:
    def __init__(self, seq, bags, text_dev, image_dev, users, width, rank, down_dev, store, cols):
        self.seq, self.bags, self.users, self.rank, self.store = seq, bags, users, rank, store
        self.text_dev, self.image_dev, self.width, self.cols = text_dev, image_dev, width, cols
        self.rows = text_dev + image_dev
        self.chips = seq // CORES
        self.half = self.chips // 2
        self.down_dev = down_dev
        self.down_rows = round_up(2 * down_dev, 16)
        self.parts = width // cols
        self.heads = cols // (3 * HEAD_DIM)
        self.wide = self.heads * HEAD_DIM
        self.lanes = round_up(self.rows, 128)
        self.groups = [[("own", 0)]]
        for hop in range(1, self.chips):
            if 2 * hop < self.chips:
                self.groups[0] += [("near", hop), ("far", hop)]
            else:
                self.groups.append([("both", hop)])

    def on_cores(self, pairs, cross=0):
        return [
            (CORES * a + c, CORES * b + (c ^ cross)) for a, b in pairs for c in range(CORES)
        ]


def place_of(plan, slot, half, seq_index):
    chip, core = seq_index // CORES, seq_index % CORES
    kind, hop = slot
    if kind == "own":
        source, lead = chip, core
    elif kind == "near":
        source, lead = jnp.where(core == 1, chip - hop, chip + hop), core
    elif kind == "far":
        source, lead = jnp.where(core == 1, chip + hop, chip - hop), 1 - core
    else:
        low = chip >= hop
        source, lead = jnp.where(low, chip - hop, chip + hop), jnp.where(low, 1, 0)
    valid = (source >= 0) & (source < plan.chips)
    source = jnp.clip(source, 0, plan.chips - 1)
    return source * CORES + (lead if half == 0 else 1 - lead), valid


def refs_per_half(slots):
    return CORES if slots[0][0] == "both" else 1


def is_passed(plan, slot, seq_index):
    chip, core = seq_index // CORES, seq_index % CORES
    return jnp.where(core == 1, chip >= slot[1], chip + slot[1] < plan.chips)


def image_seg_of(position, lengths_ref, users):
    seg = jnp.zeros_like(position)
    end = jnp.int32(0)
    for user in range(users):
        for _ in range(2):
            end = end + lengths_ref[0, user]
            seg = seg + (position >= end).astype(jnp.int32)
    return seg


def user_keys(plan, bag, store_row_ref, adapter_ref):
    return [
        lax.bitwise_xor(store_row_ref[adapter_ref[bag, user]] // plan.store, bag)
        for user in range(plan.users)
    ]


def hidden_kernel(plan, lengths_ref, text_ref, image_ref, mod_ref, out_ref):
    seq_index = lax.axis_index("seq")
    segs = mod_ref.shape[0]

    def normed(rows):
        values = rows.astype(jnp.float32)
        centre = values - jnp.mean(values, axis=-1, keepdims=True)
        spread = jnp.mean(centre * centre, axis=-1, keepdims=True)
        return centre * lax.rsqrt(spread + 1e-06)

    def image_step(step, _):
        rows = pl.ds(pl.multiple_of(step * ROW_STEP, ROW_STEP), ROW_STEP)
        place = seq_index * plan.image_dev + step * ROW_STEP
        position = place + lax.broadcasted_iota(jnp.int32, (ROW_STEP, 1), 0)
        seg = image_seg_of(position, lengths_ref, plan.users)
        base = normed(image_ref[rows, :])
        shift = jnp.zeros_like(base)
        scale = jnp.zeros_like(base)
        for one in range(segs):
            hit = seg == one
            shift = jnp.where(hit, mod_ref[one, 1, 0:1, :], shift)
            scale = jnp.where(hit, mod_ref[one, 1, 1:2, :], scale)
        target = pl.ds(pl.multiple_of(plan.text_dev + step * ROW_STEP, ROW_STEP), ROW_STEP)
        out_ref[target, :] = ((1.0 + scale) * base + shift).astype(jnp.bfloat16)
        return 0

    lax.fori_loop(0, plan.image_dev // ROW_STEP, image_step, 0)

    def text_step(step, _):
        rows = pl.ds(pl.multiple_of(step * ROW_STEP, ROW_STEP), ROW_STEP)
        seg = (seq_index * plan.text_dev + step * ROW_STEP) // TEXT
        shift = mod_ref[seg, 0, 0:1, :]
        scale = mod_ref[seg, 0, 1:2, :]
        out_ref[rows, :] = ((1.0 + scale) * normed(text_ref[rows, :]) + shift).astype(jnp.bfloat16)
        return 0

    lax.fori_loop(0, plan.text_dev // ROW_STEP, text_step, 0)


def hidden_rows(plan, lengths, text_rows, image_rows, modulation):
    return pl.pallas_call(
        functools.partial(hidden_kernel, plan),
        out_shape=jax.ShapeDtypeStruct((plan.rows, plan.width), jnp.bfloat16),
        in_specs=[SMEM(), VMEM(), VMEM(), VMEM()],
        out_specs=VMEM(),
        name="hidden_rows",
    )(lengths, text_rows, image_rows, modulation)


def pack_kernel(plan, store_row_ref, adapter_ref, down_hbm, up_hbm, *rest):
    outs, ups, rest = rest[: plan.bags], rest[plan.bags : 2 * plan.bags], rest[2 * plan.bags :]
    down, up, down_sem, up_sem = rest
    bag = lax.axis_index("bag")
    copies = []
    for hop in range(plan.bags):
        target = lax.bitwise_xor(bag, hop)
        place = jnp.int32(0)
        for user in range(plan.users):
            row = store_row_ref[adapter_ref[target, user]]
            place = jnp.where(row // plan.store == bag, row % plan.store, place)
        one = pltpu.make_async_copy(down_hbm.at[place], down.at[hop], down_sem.at[hop])
        two = pltpu.make_async_copy(up_hbm.at[place], up.at[hop], up_sem.at[hop])
        one.start()
        two.start()
        copies.append((one, two))
    pad = plan.down_rows - 2 * plan.down_dev
    for hop in range(plan.bags):
        copies[hop][0].wait()
        for part in range(plan.parts):
            lanes = slice(part * plan.cols, (part + 1) * plan.cols)
            rows = [down[hop, t, :, lanes].astype(jnp.float32) for t in range(2)]
            if pad:
                rows.append(jnp.zeros((pad, plan.cols), jnp.float32))
            spot = slice(part * plan.down_rows, (part + 1) * plan.down_rows)
            outs[hop][spot, :] = jnp.concatenate(rows, axis=0).astype(jnp.bfloat16)
        copies[hop][1].wait()
        for t in range(2):
            ups[hop][t * plan.rank : (t + 1) * plan.rank, :] = up[hop, t]


def packed_adapters(plan, store_row, user_adapter, store_down, store_up):
    sizes = (plan.parts * plan.down_rows, 2 * plan.rank)
    return pl.pallas_call(
        functools.partial(pack_kernel, plan),
        out_shape=[
            jax.ShapeDtypeStruct((rows, plan.cols), jnp.bfloat16)
            for rows in sizes
            for _ in range(plan.bags)
        ],
        in_specs=[SMEM(), SMEM(), HBM(), HBM()],
        out_specs=[VMEM()] * (2 * plan.bags),
        scratch_shapes=[
            pltpu.VMEM((plan.bags,) + store_down.shape[1:], jnp.bfloat16),
            pltpu.VMEM((plan.bags,) + store_up.shape[1:], jnp.bfloat16),
            pltpu.SemaphoreType.DMA((plan.bags,)),
            pltpu.SemaphoreType.DMA((plan.bags,)),
        ],
        name="packed_adapters",
    )(store_row, user_adapter, store_down, store_up)


def project_kernel(plan, slots, *refs):
    blocks, (weight_ref, text_out, image_out, texts, images) = refs[:-5], refs[-5:]
    text_dev, image_dev, each = plan.text_dev, plan.image_dev, refs_per_half(slots)

    def take(at, block):
        texts[at * text_dev : (at + 1) * text_dev, :] = block[:text_dev, :]
        images[at * image_dev : (at + 1) * image_dev, :] = block[text_dev:, :]

    if each == 1:
        for at, block in enumerate(blocks):
            take(at, block)
    else:
        passed = is_passed(plan, slots[0], lax.axis_index("seq"))
        for choice in range(2):

            @pl.when(passed if choice == 0 else jnp.logical_not(passed))
            def _():
                for at in range(CORES):
                    take(at, blocks[2 * at + choice])

    text_out[...] = jnp.dot(texts[...], weight_ref[0], preferred_element_type=jnp.float32)
    image_out[...] = jnp.dot(images[...], weight_ref[1], preferred_element_type=jnp.float32)


def project(plan, slots, blocks, head_weight):
    count = CORES * len(slots)
    sizes = (count * plan.text_dev, count * plan.image_dev)
    return pl.pallas_call(
        functools.partial(project_kernel, plan, slots),
        out_shape=tuple(jax.ShapeDtypeStruct((size, plan.cols), jnp.float32) for size in sizes),
        in_specs=[VMEM()] * (len(blocks) + 1),
        out_specs=(VMEM(), VMEM()),
        scratch_shapes=[pltpu.VMEM((size, plan.width), jnp.bfloat16) for size in sizes],
        compiler_params=PARAMS,
        cost_estimate=pl.CostEstimate(
            flops=2 * sum(sizes) * plan.width * plan.cols,
            bytes_accessed=2 * sum(sizes) * plan.width,
            transcendentals=0,
        ),
    )(*blocks, head_weight)


def lane_keys(plan, lengths_ref, keys, place):
    lane = lax.broadcasted_iota(jnp.int32, (1, plan.lanes), 1)
    is_text = lane < plan.text_dev
    text_seg = (place * plan.text_dev + lane) // TEXT
    image_at = place * plan.image_dev + lane - plan.text_dev
    seg = jnp.where(is_text, text_seg, image_seg_of(image_at, lengths_ref, plan.users))
    key = jnp.zeros_like(lane)
    for user in range(plan.users):
        key = jnp.where(seg // 2 == user, keys[user], key)
    return key, is_text


def rank_kernel(plan, slots, lengths_ref, store_row_ref, adapter_ref, *refs):
    halves = CORES * len(slots)
    downs, refs = refs[: plan.half], refs[plan.half :]
    each = refs_per_half(slots)
    blocks, refs = refs[: each * halves], refs[each * halves :]
    before, (out_ref, stacked) = refs[:-2], refs[-2:]
    for one in before:
        out_ref[...] = one[...]
    bag, seq_index = lax.axis_index("bag"), lax.axis_index("seq")
    chip = seq_index // CORES
    passed = is_passed(plan, slots[0], seq_index)
    keys = user_keys(plan, bag, store_row_ref, adapter_ref)
    tall = plan.bags * plan.down_rows
    for index, down_ref in enumerate(downs):
        for part in range(plan.parts):
            lanes = slice(part * plan.cols, (part + 1) * plan.cols)
            stacked[index * tall : (index + 1) * tall, lanes] = down_ref[part]
    for at in range(halves):
        place, valid = place_of(plan, slots[at // CORES], at % CORES, seq_index)
        block = blocks[each * at][...]
        if each > 1:
            block = jnp.where(passed, block, blocks[each * at + 1][...])
        found = lax.dot_general(block, stacked[...], NT, preferred_element_type=jnp.float32)
        found = jnp.transpose(found)
        if plan.rows < plan.lanes:
            pad = jnp.zeros((found.shape[0], plan.lanes - plan.rows), jnp.float32)
            found = jnp.concatenate([found, pad], axis=1)
        key, is_text = lane_keys(plan, lengths_ref, keys, place)
        for index in range(plan.half):
            total = jnp.zeros((plan.down_dev, plan.lanes), jnp.float32)
            for hop in range(plan.bags):
                top = index * tall + hop * plan.down_rows
                text_part = found[top : top + plan.down_dev]
                image_part = found[top + plan.down_dev : top + 2 * plan.down_dev]
                total = total + jnp.where(
                    key == hop, jnp.where(is_text, text_part, image_part), 0.0
                )
            spot = jnp.where(chip < plan.half, plan.half - 1 - index, index)

            @pl.when(valid)
            def _():
                out_ref[spot, place] = total.astype(jnp.bfloat16)


def rank_parts(plan, slots, lengths, store_row, user_adapter, downs, blocks, before):
    before = [] if before is None else [before]
    each = plan.bags * plan.down_rows
    rows = plan.rows * len(blocks)
    return pl.pallas_call(
        functools.partial(rank_kernel, plan, slots),
        out_shape=jax.ShapeDtypeStruct(
            (plan.half, plan.seq, plan.down_dev, plan.lanes), jnp.bfloat16
        ),
        in_specs=[SMEM()] * 3 + [VMEM()] * (len(downs) + len(blocks) + len(before)),
        out_specs=VMEM(),
        scratch_shapes=[pltpu.VMEM((len(downs) * each, plan.width), jnp.bfloat16)],
        compiler_params=PARAMS,
        cost_estimate=pl.CostEstimate(
            flops=4 * rows * plan.width * len(downs) * each,
            bytes_accessed=2 * rows * plan.width,
            transcendentals=0,
        ),
        name="rank_parts",
    )(lengths, store_row, user_adapter, *downs, *blocks, *before)


def head_normed(values, gain_row):
    spread = jnp.mean(values * values, axis=-1, keepdims=True)
    return (values * lax.rsqrt(spread + 1e-06) * gain_row).astype(jnp.bfloat16)


def write_heads(plan, mixed_of, gain_ref, stream, out_ref, rows):
    for head in range(plan.heads):
        for which in range(3):
            first = (3 * head + which) * HEAD_DIM
            mixed = mixed_of(slice(first, first + HEAD_DIM))
            if which < 2:
                mixed = head_normed(mixed, gain_ref[stream, which : which + 1, :])
            lanes = slice(head * HEAD_DIM, (head + 1) * HEAD_DIM)
            out_ref[which, rows, lanes] = mixed.astype(jnp.bfloat16)


def early_kernel(plan, groups, lengths_ref, store_row_ref, adapter_ref, gain_ref, *refs):
    ranks, refs = refs[: plan.half], refs[plan.half :]
    packs, refs = refs[: plan.bags], refs[plan.bags :]
    plains, refs = refs[: 2 * len(groups)], refs[2 * len(groups) :]
    text_heads, image_heads, text_last, image_last, ranks_ref, spread, ups, adjust = refs
    bag, seq_index = lax.axis_index("bag"), lax.axis_index("seq")
    chip, core = seq_index // CORES, seq_index % CORES
    upper = (chip >= plan.half).astype(jnp.int32)
    reach = jnp.where(chip < plan.half, plan.half - 1 - chip, chip - plan.half)
    for hop in range(plan.half):

        @pl.when(reach == hop)
        def _():
            ranks_ref[...] = ranks[hop][...]

    keys = user_keys(plan, bag, store_row_ref, adapter_ref)
    for place in range(plan.seq):
        key, _ = lane_keys(plan, lengths_ref, keys, place)
        lanes = slice(place * plan.lanes, (place + 1) * plan.lanes)
        for side in range(2):
            for lead in range(CORES):
                for index in range(plan.half):
                    rows = ranks_ref[
                        lax.bitwise_xor(upper, side), lax.bitwise_xor(core, lead), index, place
                    ].astype(jnp.float32)
                    first = ((side * plan.half + index) * CORES + lead) * plan.down_dev
                    for hop in range(plan.bags):
                        top = hop * plan.rank + first
                        spread[top : top + plan.down_dev, lanes] = jnp.where(key == hop, rows, 0.0)
    for stream in range(2):
        for hop in range(plan.bags):
            ups[hop * plan.rank : (hop + 1) * plan.rank, :] = packs[hop][
                stream * plan.rank : (stream + 1) * plan.rank, :
            ]
        adjust[...] = lax.dot_general(
            spread[...].astype(jnp.bfloat16), ups[...], TN, preferred_element_type=jnp.float32
        )
        size = plan.text_dev if stream == 0 else plan.image_dev
        skip = 0 if stream == 0 else plan.text_dev
        out_ref = text_heads if stream == 0 else image_heads
        last_ref = text_last if stream == 0 else image_last

        def rows_of(place):
            return pl.ds(pl.multiple_of(place * plan.lanes + skip, 32), size)

        for group_at, group in enumerate(groups):
            plain = plains[2 * group_at + stream]
            for at in range(CORES * len(group)):
                place, valid = place_of(plan, group[at // CORES], at % CORES, seq_index)

                @pl.when(valid)
                def _():
                    write_heads(
                        plan,
                        lambda lanes: plain[at * size : (at + 1) * size, lanes]
                        + adjust[rows_of(place), lanes],
                        gain_ref,
                        stream,
                        out_ref,
                        pl.ds(pl.multiple_of(place * size, size), size),
                    )

        for half in range(CORES):
            place, _ = place_of(plan, plan.groups[-1][0], half, seq_index)
            last_ref[half * size : (half + 1) * size, :] = adjust[rows_of(place), :]


def early_heads(plan, groups, lengths, store_row, user_adapter, norm_gain, ranks, packs, plains):
    total = (plan.seq * plan.text_dev, plan.seq * plan.image_dev)
    last = (CORES * plan.text_dev, CORES * plan.image_dev)
    scratch = 4 * plan.seq * plan.lanes * (plan.bags * plan.rank + plan.cols)
    return pl.pallas_call(
        functools.partial(early_kernel, plan, groups),
        out_shape=tuple(jax.ShapeDtypeStruct((3, n, plan.wide), jnp.bfloat16) for n in total)
        + tuple(jax.ShapeDtypeStruct((n, plan.cols), jnp.float32) for n in last),
        in_specs=[SMEM()] * 3 + [VMEM()] * (1 + plan.half + plan.bags + len(plains)),
        out_specs=(VMEM(),) * 4,
        scratch_shapes=[
            pltpu.VMEM(ranks[0].shape, jnp.bfloat16),
            pltpu.VMEM((plan.bags * plan.rank, plan.seq * plan.lanes), jnp.float32),
            pltpu.VMEM((plan.bags * plan.rank, plan.cols), jnp.bfloat16),
            pltpu.VMEM((plan.seq * plan.lanes, plan.cols), jnp.float32),
        ],
        compiler_params=pltpu.CompilerParams(vmem_limit_bytes=max(VMEM_GRANT, 2 * scratch)),
        cost_estimate=pl.CostEstimate(
            flops=4 * plan.seq * plan.lanes * plan.bags * plan.rank * plan.cols,
            bytes_accessed=8 * sum(total) * plan.cols,
            transcendentals=0,
        ),
        name="early_heads",
    )(lengths, store_row, user_adapter, norm_gain, *ranks, *packs, *plains)


def attend_kernel(plan, lengths_ref, gain_ref, *refs):
    text_in, image_in, text_plain, image_plain, text_adjust, image_adjust = refs[:6]
    out_ref, text_heads, image_heads = refs[6:]
    seq_index = lax.axis_index("seq")
    factor = 1.0 / math.sqrt(HEAD_DIM)
    text_heads[...] = text_in[...]
    image_heads[...] = image_in[...]
    for stream in range(2):
        plain = text_plain if stream == 0 else image_plain
        adjust = text_adjust if stream == 0 else image_adjust
        size = plan.text_dev if stream == 0 else plan.image_dev
        for half in range(CORES):
            place, valid = place_of(plan, plan.groups[-1][0], half, seq_index)
            rows = slice(half * size, (half + 1) * size)

            @pl.when(valid)
            def _():
                write_heads(
                    plan,
                    lambda lanes: plain[rows, lanes] + adjust[rows, lanes],
                    gain_ref,
                    stream,
                    text_heads if stream == 0 else image_heads,
                    pl.ds(pl.multiple_of(place * size, size), size),
                )

    text_total, image_total = plan.seq * plan.text_dev, plan.seq * plan.image_dev
    image_seg = functools.partial(image_seg_of, lengths_ref=lengths_ref, users=plan.users)
    text_cols = lax.broadcasted_iota(jnp.int32, (1, text_total), 1) // TEXT
    image_cols = image_seg(lax.broadcasted_iota(jnp.int32, (1, image_total), 1))
    image_rows = image_seg(lax.broadcasted_iota(jnp.int32, (image_total, 1), 0))
    step = TEXT

    def softmax(scores, hits):
        scores = [jnp.where(hit, one * factor, -1e30) for one, hit in zip(scores, hits)]
        tops = [jnp.max(one, axis=1, keepdims=True) for one in scores]
        top = functools.reduce(jnp.maximum, tops)
        weights = [jnp.exp(one - top) for one in scores]
        total = sum(jnp.sum(one, axis=1, keepdims=True) for one in weights)
        inverse = 1.0 / total
        return [(one * inverse).astype(jnp.bfloat16) for one in weights]

    def pair(queries, keys):
        return lax.dot_general(queries, keys, NT, preferred_element_type=jnp.float32)

    def mix(probs, values):
        found = [
            jnp.dot(one, value, preferred_element_type=jnp.float32)
            for one, value in zip(probs, values)
        ]
        return sum(found).astype(jnp.bfloat16)

    for head in range(plan.heads):
        lanes = slice(head * HEAD_DIM, (head + 1) * HEAD_DIM)
        image_keys, image_values = image_heads[1, :, lanes], image_heads[2, :, lanes]
        for seg in range(text_total // step):
            rows = slice(seg * step, (seg + 1) * step)
            queries = text_heads[0, rows, lanes]
            near = pair(queries, text_heads[1, rows, lanes]) * factor
            far = pair(queries, image_keys)
            far = jnp.where(image_cols == seg, far * factor, -1e30)
            top = jnp.maximum(
                jnp.max(near, axis=1, keepdims=True), jnp.max(far, axis=1, keepdims=True)
            )
            near, far = jnp.exp(near - top), jnp.exp(far - top)
            total = jnp.sum(near, axis=1, keepdims=True) + jnp.sum(far, axis=1, keepdims=True)
            inverse = 1.0 / total
            probs = [(one * inverse).astype(jnp.bfloat16) for one in (near, far)]
            place, inner = divmod(seg * step, plan.text_dev)
            out_ref[place, inner : inner + step, lanes] = mix(
                probs, (text_heads[2, rows, lanes], image_values)
            )
        queries = image_heads[0, :, lanes]
        probs = softmax(
            (pair(queries, image_keys), pair(queries, text_heads[1, :, lanes])),
            (image_rows == image_cols, image_rows == text_cols),
        )
        result = mix(probs, (image_values, text_heads[2, :, lanes]))
        for place in range(plan.seq):
            out_ref[place, plan.text_dev :, lanes] = result[
                place * plan.image_dev : (place + 1) * plan.image_dev, :
            ]


def attention(plan, lengths, norm_gain, arrays):
    text_total, image_total = plan.seq * plan.text_dev, plan.seq * plan.image_dev
    return pl.pallas_call(
        functools.partial(attend_kernel, plan),
        out_shape=jax.ShapeDtypeStruct((plan.seq, plan.rows, plan.wide), jnp.bfloat16),
        in_specs=[SMEM()] + [VMEM()] * (1 + len(arrays)),
        out_specs=VMEM(),
        scratch_shapes=[
            pltpu.VMEM((3, text_total, plan.wide), jnp.bfloat16),
            pltpu.VMEM((3, image_total, plan.wide), jnp.bfloat16),
        ],
        compiler_params=PARAMS,
        name="attention",
    )(lengths, norm_gain, *arrays)


def place_kernel(plan, pieces, text_out, image_out):
    for place in range(plan.seq):
        lanes = slice(place * plan.wide, (place + 1) * plan.wide)
        text_out[:, lanes] = pieces[place, : plan.text_dev, :]
        image_out[:, lanes] = pieces[place, plan.text_dev :, :]


def placed(plan, pieces):
    sizes = (plan.text_dev, plan.image_dev)
    return pl.pallas_call(
        functools.partial(place_kernel, plan),
        out_shape=tuple(
            jax.ShapeDtypeStruct((n, plan.seq * plan.wide), jnp.bfloat16) for n in sizes
        ),
        in_specs=[VMEM()],
        out_specs=(VMEM(), VMEM()),
        compiler_params=PARAMS,
        name="placed",
    )(pieces)


def steps(
    text_rows,
    image_rows,
    modulation,
    head_weight,
    norm_gain,
    store_down,
    store_up,
    store_row,
    user_adapter,
    image_lengths,
):
    seq, bags = lax.axis_size("seq"), lax.axis_size("bag")
    plan = Plan(
        seq,
        bags,
        text_rows.shape[0],
        image_rows.shape[0],
        image_lengths.shape[1],
        text_rows.shape[1],
        store_up.shape[2],
        store_down.shape[2],
        store_down.shape[0],
        head_weight.shape[2],
    )
    swap = plan.on_cores([(z, z) for z in range(plan.chips)], 1)

    hidden = hidden_rows(plan, image_lengths, text_rows, image_rows, modulation)
    blocks = {("own", 0, 0): hidden, ("own", 0, 1): lax.ppermute(hidden, "seq", swap)}
    passing = [blocks["own", 0, 0], blocks["own", 0, 1]]
    for hop in range(1, plan.chips):
        up = [(2 * z + 1, 2 * z + 3) for z in range(hop - 1, plan.chips - 1)]
        down = [(2 * z, 2 * z - 2) for z in range(1, plan.chips - hop + 1)]
        for half in range(CORES):
            passing[half] = lax.ppermute(passing[half], "seq", up + down)
            other = lax.ppermute(passing[half], "seq", swap)
            if 2 * hop < plan.chips:
                blocks["near", hop, half] = passing[half]
                blocks["far", hop, half] = other
            else:
                blocks["both", hop, half] = (passing[half], other)

    packs = packed_adapters(plan, store_row, user_adapter, store_down, store_up)
    arrived = {}
    for kind, sent in (("down", packs[:bags]), ("up", packs[bags:])):
        arrived[kind] = [sent[0]] + [
            lax.ppermute(sent[hop], "bag", [(b, b ^ hop) for b in range(bags)])
            for hop in range(1, bags)
        ]
    down_shape = (plan.parts, plan.down_rows, plan.cols)
    down_own = jnp.concatenate([one.reshape(down_shape) for one in arrived["down"]], axis=1)
    low, high = plan.half - 1, plan.half
    downs = [down_own] + [
        lax.ppermute(down_own, "seq", plan.on_cores([(low - hop, low), (high + hop, high)]))
        for hop in range(1, plan.half)
    ]

    def blocks_of(slots):
        found = [blocks[kind, hop, half] for kind, hop in slots for half in range(CORES)]
        return [one for pick in found for one in (pick if isinstance(pick, tuple) else (pick,))]

    plains = []
    for group in plan.groups:
        plains.append(project(plan, group, blocks_of(group), head_weight))
    scalars = (image_lengths, store_row, user_adapter)
    ranks = None
    for group in plan.groups[:2]:
        ranks = rank_parts(plan, group, *scalars, downs, blocks_of(group), ranks)
    ranks = jnp.stack([ranks, lax.ppermute(ranks, "seq", swap)])
    other = lax.ppermute(ranks, "seq", plan.on_cores([(low, high), (high, low)]))
    ranks = jnp.stack([ranks, other])
    ranks = [ranks] + [
        lax.ppermute(ranks, "seq", plan.on_cores([(low, low - hop), (high, high + hop)]))
        for hop in range(1, plan.half)
    ]

    arrays = early_heads(
        plan,
        plan.groups[:-1],
        *scalars,
        norm_gain,
        ranks,
        arrived["up"],
        [one for pair in plains[:-1] for one in pair],
    )
    outs = attention(
        plan, image_lengths, norm_gain, list(arrays[:2]) + list(plains[-1]) + list(arrays[2:])
    )
    pieces = lax.all_to_all(outs, "seq", split_axis=0, concat_axis=0, tiled=True)
    return placed(plan, pieces)


def solution(mesh):
    in_specs = (
        P(("bag", "seq"), None),
        P(("bag", "seq"), None),
        P("bag", None, None, None),
        P(None, None, "seq"),
        P(),
        P("bag", None, "seq", None),
        P("bag", None, None, "seq"),
        P(),
        P(),
        P("bag", None),
    )
    out_specs = (P(("bag", "seq"), None), P(("bag", "seq"), None))
    return jax.shard_map(steps, mesh=mesh, in_specs=in_specs, out_specs=out_specs, check_vma=False)
```

```python
import functools
import math

import jax
import jax.numpy as jnp
from jax import lax
from jax.experimental import pallas as pl
from jax.experimental.pallas import tpu as pltpu
from jax.sharding import PartitionSpec as P


HEAD_DIM = 128
TEXT = 64
CORES = 2
ROW_STEP = 16


VMEM_GRANT = 26 << 20
PARAMS = pltpu.CompilerParams(vmem_limit_bytes=VMEM_GRANT)

SMEM = functools.partial(pl.BlockSpec, memory_space=pltpu.SMEM)
VMEM = functools.partial(pl.BlockSpec, memory_space=pltpu.VMEM)
HBM = functools.partial(pl.BlockSpec, memory_space=pltpu.HBM)
NT = (((1,), (1,)), ((), ()))


def round_up(value, step):
    return -(-value // step) * step


class Plan:
    def __init__(self, seq, bags, text_dev, image_dev, users, width, rank, down_dev, store, cols):
        self.seq, self.bags, self.users, self.rank, self.store = seq, bags, users, rank, store
        self.text_dev, self.image_dev, self.width, self.cols = text_dev, image_dev, width, cols
        self.rows = text_dev + image_dev
        self.chips = seq // CORES
        self.half = self.chips // 2
        self.down_dev = down_dev
        self.down_rows = round_up(2 * down_dev, 16)
        self.parts = width // cols
        self.heads = cols // (3 * HEAD_DIM)
        self.wide = self.heads * HEAD_DIM
        self.lanes = round_up(self.rows, 128)
        self.groups = [[("own", 0)]]
        for hop in range(1, self.chips):
            if 2 * hop < self.chips:
                self.groups[0] += [("near", hop), ("far", hop)]
            else:
                self.groups.append([("both", hop)])

    def on_cores(self, pairs, cross=0):
        return [
            (CORES * a + c, CORES * b + (c ^ cross)) for a, b in pairs for c in range(CORES)
        ]


def place_of(plan, slot, half, seq_index):
    chip, core = seq_index // CORES, seq_index % CORES
    kind, hop = slot
    if kind == "own":
        source, lead = chip, core
    elif kind == "near":
        source, lead = jnp.where(core == 1, chip - hop, chip + hop), core
    elif kind == "far":
        source, lead = jnp.where(core == 1, chip + hop, chip - hop), 1 - core
    else:
        low = chip >= hop
        source, lead = jnp.where(low, chip - hop, chip + hop), jnp.where(low, 1, 0)
    valid = (source >= 0) & (source < plan.chips)
    source = jnp.clip(source, 0, plan.chips - 1)
    return source * CORES + (lead if half == 0 else 1 - lead), valid


def refs_per_half(slots):
    return CORES if slots[0][0] == "both" else 1


def is_passed(plan, slot, seq_index):
    chip, core = seq_index // CORES, seq_index % CORES
    return jnp.where(core == 1, chip >= slot[1], chip + slot[1] < plan.chips)


def image_seg_of(position, lengths_ref, users):
    seg = jnp.zeros_like(position)
    end = jnp.int32(0)
    for user in range(users):
        for _ in range(2):
            end = end + lengths_ref[0, user]
            seg = seg + (position >= end).astype(jnp.int32)
    return seg


def user_keys(plan, bag, store_row_ref, adapter_ref):
    return [
        lax.bitwise_xor(store_row_ref[adapter_ref[bag, user]] // plan.store, bag)
        for user in range(plan.users)
    ]


def hidden_kernel(plan, lengths_ref, text_ref, image_ref, mod_ref, out_ref):
    seq_index = lax.axis_index("seq")
    segs = mod_ref.shape[0]

    def normed(rows):
        values = rows.astype(jnp.float32)
        centre = values - jnp.mean(values, axis=-1, keepdims=True)
        spread = jnp.mean(centre * centre, axis=-1, keepdims=True)
        return centre * lax.rsqrt(spread + 1e-06)

    def image_step(step, _):
        rows = pl.ds(pl.multiple_of(step * ROW_STEP, ROW_STEP), ROW_STEP)
        place = seq_index * plan.image_dev + step * ROW_STEP
        position = place + lax.broadcasted_iota(jnp.int32, (ROW_STEP, 1), 0)
        seg = image_seg_of(position, lengths_ref, plan.users)
        base = normed(image_ref[rows, :])
        shift = jnp.zeros_like(base)
        scale = jnp.zeros_like(base)
        for one in range(segs):
            hit = seg == one
            shift = jnp.where(hit, mod_ref[one, 1, 0:1, :], shift)
            scale = jnp.where(hit, mod_ref[one, 1, 1:2, :], scale)
        target = pl.ds(pl.multiple_of(plan.text_dev + step * ROW_STEP, ROW_STEP), ROW_STEP)
        out_ref[target, :] = ((1.0 + scale) * base + shift).astype(jnp.bfloat16)
        return 0

    lax.fori_loop(0, plan.image_dev // ROW_STEP, image_step, 0)

    def text_step(step, _):
        rows = pl.ds(pl.multiple_of(step * ROW_STEP, ROW_STEP), ROW_STEP)
        seg = (seq_index * plan.text_dev + step * ROW_STEP) // TEXT
        shift = mod_ref[seg, 0, 0:1, :]
        scale = mod_ref[seg, 0, 1:2, :]
        out_ref[rows, :] = ((1.0 + scale) * normed(text_ref[rows, :]) + shift).astype(jnp.bfloat16)
        return 0

    lax.fori_loop(0, plan.text_dev // ROW_STEP, text_step, 0)


def hidden_rows(plan, lengths, text_rows, image_rows, modulation):
    return pl.pallas_call(
        functools.partial(hidden_kernel, plan),
        out_shape=jax.ShapeDtypeStruct((plan.rows, plan.width), jnp.bfloat16),
        in_specs=[SMEM(), VMEM(), VMEM(), VMEM()],
        out_specs=VMEM(),
        name="hidden_rows",
    )(lengths, text_rows, image_rows, modulation)


def pack_kernel(plan, store_row_ref, adapter_ref, down_hbm, up_hbm, *rest):
    outs, ups, rest = rest[: plan.bags], rest[plan.bags : 2 * plan.bags], rest[2 * plan.bags :]
    down, up, down_sem, up_sem = rest
    bag = lax.axis_index("bag")
    copies = []
    for hop in range(plan.bags):
        target = lax.bitwise_xor(bag, hop)
        place = jnp.int32(0)
        for user in range(plan.users):
            row = store_row_ref[adapter_ref[target, user]]
            place = jnp.where(row // plan.store == bag, row % plan.store, place)
        one = pltpu.make_async_copy(down_hbm.at[place], down.at[hop], down_sem.at[hop])
        two = pltpu.make_async_copy(up_hbm.at[place], up.at[hop], up_sem.at[hop])
        one.start()
        two.start()
        copies.append((one, two))
    pad = plan.down_rows - 2 * plan.down_dev
    for hop in range(plan.bags):
        copies[hop][0].wait()
        for part in range(plan.parts):
            lanes = slice(part * plan.cols, (part + 1) * plan.cols)
            rows = [down[hop, t, :, lanes].astype(jnp.float32) for t in range(2)]
            if pad:
                rows.append(jnp.zeros((pad, plan.cols), jnp.float32))
            spot = slice(part * plan.down_rows, (part + 1) * plan.down_rows)
            outs[hop][spot, :] = jnp.concatenate(rows, axis=0).astype(jnp.bfloat16)
        copies[hop][1].wait()
        for t in range(2):
            ups[hop][t * plan.rank : (t + 1) * plan.rank, :] = up[hop, t]


def packed_adapters(plan, store_row, user_adapter, store_down, store_up):
    sizes = (plan.parts * plan.down_rows, 2 * plan.rank)
    return pl.pallas_call(
        functools.partial(pack_kernel, plan),
        out_shape=[
            jax.ShapeDtypeStruct((rows, plan.cols), jnp.bfloat16)
            for rows in sizes
            for _ in range(plan.bags)
        ],
        in_specs=[SMEM(), SMEM(), HBM(), HBM()],
        out_specs=[VMEM()] * (2 * plan.bags),
        scratch_shapes=[
            pltpu.VMEM((plan.bags,) + store_down.shape[1:], jnp.bfloat16),
            pltpu.VMEM((plan.bags,) + store_up.shape[1:], jnp.bfloat16),
            pltpu.SemaphoreType.DMA((plan.bags,)),
            pltpu.SemaphoreType.DMA((plan.bags,)),
        ],
        name="packed_adapters",
    )(store_row, user_adapter, store_down, store_up)


def project_kernel(plan, slots, *refs):
    blocks, (weight_ref, text_out, image_out, texts, images) = refs[:-5], refs[-5:]
    text_dev, image_dev, each = plan.text_dev, plan.image_dev, refs_per_half(slots)

    def take(at, block):
        texts[at * text_dev : (at + 1) * text_dev, :] = block[:text_dev, :]
        images[at * image_dev : (at + 1) * image_dev, :] = block[text_dev:, :]

    if each == 1:
        for at, block in enumerate(blocks):
            take(at, block)
    else:
        passed = is_passed(plan, slots[0], lax.axis_index("seq"))
        for choice in range(2):

            @pl.when(passed if choice == 0 else jnp.logical_not(passed))
            def _():
                for at in range(CORES):
                    take(at, blocks[2 * at + choice])

    text_out[...] = jnp.dot(texts[...], weight_ref[0], preferred_element_type=jnp.float32)
    image_out[...] = jnp.dot(images[...], weight_ref[1], preferred_element_type=jnp.float32)


def project(plan, slots, blocks, head_weight):
    count = CORES * len(slots)
    sizes = (count * plan.text_dev, count * plan.image_dev)
    return pl.pallas_call(
        functools.partial(project_kernel, plan, slots),
        out_shape=tuple(jax.ShapeDtypeStruct((size, plan.cols), jnp.float32) for size in sizes),
        in_specs=[VMEM()] * (len(blocks) + 1),
        out_specs=(VMEM(), VMEM()),
        scratch_shapes=[pltpu.VMEM((size, plan.width), jnp.bfloat16) for size in sizes],
        compiler_params=PARAMS,
        cost_estimate=pl.CostEstimate(
            flops=2 * sum(sizes) * plan.width * plan.cols,
            bytes_accessed=2 * sum(sizes) * plan.width,
            transcendentals=0,
        ),
    )(*blocks, head_weight)


def lane_keys(plan, lengths_ref, keys, place):
    lane = lax.broadcasted_iota(jnp.int32, (1, plan.lanes), 1)
    is_text = lane < plan.text_dev
    text_seg = (place * plan.text_dev + lane) // TEXT
    image_at = place * plan.image_dev + lane - plan.text_dev
    seg = jnp.where(is_text, text_seg, image_seg_of(image_at, lengths_ref, plan.users))
    key = jnp.zeros_like(lane)
    for user in range(plan.users):
        key = jnp.where(seg // 2 == user, keys[user], key)
    return key, is_text


def rank_kernel(plan, slots, lengths_ref, store_row_ref, adapter_ref, *refs):
    halves = CORES * len(slots)
    each = refs_per_half(slots)
    first = slots[0][0] == "own"
    given = plan.half if first else 2
    downs, refs = refs[:given], refs[given:]
    blocks, refs = refs[: each * halves], refs[each * halves :]
    if first:
        out_ref, turned, stacked = refs
    else:
        (out_ref,), (turned, before) = refs, downs
        out_ref[...] = before[...]
    bag, seq_index = lax.axis_index("bag"), lax.axis_index("seq")
    chip = seq_index // CORES
    passed = is_passed(plan, slots[0], seq_index)
    keys = user_keys(plan, bag, store_row_ref, adapter_ref)
    tall = plan.bags * plan.down_rows
    for part in range(plan.parts if first else 0):
        lanes = slice(part * plan.cols, (part + 1) * plan.cols)
        for index, down_ref in enumerate(downs):
            stacked[index * tall : (index + 1) * tall, :] = down_ref[part].astype(jnp.float32)
        turned[lanes, :] = jnp.transpose(stacked[...]).astype(jnp.bfloat16)
    for at in range(halves):
        place, valid = place_of(plan, slots[at // CORES], at % CORES, seq_index)
        block = blocks[each * at][...]
        if each > 1:
            block = jnp.where(passed, block, blocks[each * at + 1][...])
        found = jnp.dot(block, turned[...], preferred_element_type=jnp.float32)
        found = jnp.transpose(found)
        if plan.rows < plan.lanes:
            pad = jnp.zeros((found.shape[0], plan.lanes - plan.rows), jnp.float32)
            found = jnp.concatenate([found, pad], axis=1)
        key, is_text = lane_keys(plan, lengths_ref, keys, place)
        for index in range(plan.half):
            total = jnp.zeros((plan.down_dev, plan.lanes), jnp.float32)
            for hop in range(plan.bags):
                top = index * tall + hop * plan.down_rows
                text_part = found[top : top + plan.down_dev]
                image_part = found[top + plan.down_dev : top + 2 * plan.down_dev]
                total = total + jnp.where(
                    key == hop, jnp.where(is_text, text_part, image_part), 0.0
                )
            spot = jnp.where(chip < plan.half, plan.half - 1 - index, index)

            @pl.when(valid)
            def _():
                out_ref[spot, place] = total.astype(jnp.bfloat16)


def rank_parts(plan, slots, lengths, store_row, user_adapter, downs, blocks):
    first = slots[0][0] == "own"
    tall = plan.half * plan.bags * plan.down_rows
    rows = plan.rows * CORES * len(slots)
    out_shape = [
        jax.ShapeDtypeStruct((plan.half, plan.seq, plan.down_dev, plan.lanes), jnp.bfloat16)
    ]
    if first:
        out_shape.append(jax.ShapeDtypeStruct((plan.width, tall), jnp.bfloat16))
    return pl.pallas_call(
        functools.partial(rank_kernel, plan, slots),
        out_shape=out_shape,
        in_specs=[SMEM()] * 3 + [VMEM()] * (len(downs) + len(blocks)),
        out_specs=[VMEM()] * len(out_shape),
        scratch_shapes=[pltpu.VMEM((tall, plan.cols), jnp.float32)] if first else [],
        compiler_params=PARAMS,
        cost_estimate=pl.CostEstimate(
            flops=(64 if first else 1) * rows * plan.width * tall,
            bytes_accessed=2 * rows * plan.width,
            transcendentals=0,
        ),
        name="rank_parts",
    )(lengths, store_row, user_adapter, *downs, *blocks)


def head_normed(values, gain_row):
    spread = jnp.mean(values * values, axis=-1, keepdims=True)
    return (values * lax.rsqrt(spread + 1e-06) * gain_row).astype(jnp.bfloat16)


def write_heads(plan, mixed_of, gain_ref, stream, out_ref, rows):
    for head in range(plan.heads):
        for which in range(3):
            first = (3 * head + which) * HEAD_DIM
            mixed = mixed_of(slice(first, first + HEAD_DIM))
            if which < 2:
                mixed = head_normed(mixed, gain_ref[stream, which : which + 1, :])
            lanes = slice(head * HEAD_DIM, (head + 1) * HEAD_DIM)
            out_ref[which, rows, lanes] = mixed.astype(jnp.bfloat16)


def early_kernel(plan, groups, lengths_ref, store_row_ref, adapter_ref, gain_ref, *refs):
    ranks, refs = refs[: 2 * plan.half + 1], refs[2 * plan.half + 1 :]
    packs, refs = refs[: plan.bags], refs[plan.bags :]
    plains, refs = refs[: 2 * len(groups)], refs[2 * len(groups) :]
    text_heads, image_heads, text_last, image_last, ranks_ref, spread, text_side, image_side, ups, adjust = refs
    sides = (text_side, image_side)
    bag, seq_index = lax.axis_index("bag"), lax.axis_index("seq")
    chip, core = seq_index // CORES, seq_index % CORES
    leads = []
    for side, middle in enumerate((plan.half - 1, plan.half)):
        away = jnp.abs(chip - middle)
        sender = jnp.where(away == 0, core, (chip > middle).astype(jnp.int32))
        leads.append(sender)
        for at, source in enumerate(ranks):
            hop = at if at <= plan.half else at - plan.half
            here = (away == hop) & ((sender == core) if at <= plan.half else (sender != core))

            @pl.when(here)
            def _():
                ranks_ref[side] = source[...]

    keys = user_keys(plan, bag, store_row_ref, adapter_ref)
    for place in range(plan.seq):
        key, _ = lane_keys(plan, lengths_ref, keys, place)
        for side in range(2):
            for lead in range(CORES):
                for index in range(plan.half):
                    rows = ranks_ref[
                        side, lax.bitwise_xor(leads[side], lead), index, place
                    ].astype(jnp.float32)
                    first = ((side * plan.half + index) * CORES + lead) * plan.down_dev
                    for hop in range(plan.bags):
                        top = hop * plan.rank + first
                        spread[place, top : top + plan.down_dev, :] = jnp.where(
                            key == hop, rows, 0.0
                        )
        turned = jnp.transpose(spread[place]).astype(jnp.bfloat16)
        for stream, size, skip in ((0, plan.text_dev, 0), (1, plan.image_dev, plan.text_dev)):
            sides[stream][place * size : (place + 1) * size, :] = turned[skip : skip + size, :]
    for stream in range(2):
        for hop in range(plan.bags):
            ups[hop * plan.rank : (hop + 1) * plan.rank, :] = packs[hop][
                stream * plan.rank : (stream + 1) * plan.rank, :
            ]
        size = plan.text_dev if stream == 0 else plan.image_dev
        adjust[: plan.seq * size, :] = jnp.dot(
            sides[stream][...], ups[...], preferred_element_type=jnp.float32
        )
        out_ref = text_heads if stream == 0 else image_heads
        last_ref = text_last if stream == 0 else image_last

        def rows_of(place):
            return pl.ds(pl.multiple_of(place * size, size), size)

        for group_at, group in enumerate(groups):
            plain = plains[2 * group_at + stream]
            for at in range(CORES * len(group)):
                place, valid = place_of(plan, group[at // CORES], at % CORES, seq_index)

                @pl.when(valid)
                def _():
                    write_heads(
                        plan,
                        lambda lanes: plain[at * size : (at + 1) * size, lanes]
                        + adjust[rows_of(place), lanes],
                        gain_ref,
                        stream,
                        out_ref,
                        pl.ds(pl.multiple_of(place * size, size), size),
                    )

        for half in range(CORES):
            place, _ = place_of(plan, plan.groups[-1][0], half, seq_index)
            last_ref[half * size : (half + 1) * size, :] = adjust[rows_of(place), :]


def early_heads(plan, groups, lengths, store_row, user_adapter, norm_gain, ranks, packs, plains):
    total = (plan.seq * plan.text_dev, plan.seq * plan.image_dev)
    last = (CORES * plan.text_dev, CORES * plan.image_dev)
    scratch = 4 * plan.seq * plan.lanes * (plan.bags * plan.rank + plan.cols)
    return pl.pallas_call(
        functools.partial(early_kernel, plan, groups),
        out_shape=tuple(jax.ShapeDtypeStruct((3, n, plan.wide), jnp.bfloat16) for n in total)
        + tuple(jax.ShapeDtypeStruct((n, plan.cols), jnp.float32) for n in last),
        in_specs=[SMEM()] * 3 + [VMEM()] * (1 + len(ranks) + plan.bags + len(plains)),
        out_specs=(VMEM(),) * 4,
        scratch_shapes=[
            pltpu.VMEM((2,) + ranks[0].shape, jnp.bfloat16),
            pltpu.VMEM((plan.seq, plan.bags * plan.rank, plan.lanes), jnp.float32),
            pltpu.VMEM((total[0], plan.bags * plan.rank), jnp.bfloat16),
            pltpu.VMEM((total[1], plan.bags * plan.rank), jnp.bfloat16),
            pltpu.VMEM((plan.bags * plan.rank, plan.cols), jnp.bfloat16),
            pltpu.VMEM((total[0], plan.cols), jnp.float32),
        ],
        compiler_params=pltpu.CompilerParams(vmem_limit_bytes=max(VMEM_GRANT, 2 * scratch)),
        cost_estimate=pl.CostEstimate(
            flops=4 * plan.seq * plan.lanes * plan.bags * plan.rank * plan.cols,
            bytes_accessed=8 * sum(total) * plan.cols,
            transcendentals=0,
        ),
        name="early_heads",
    )(lengths, store_row, user_adapter, norm_gain, *ranks, *packs, *plains)


def attend_kernel(plan, lengths_ref, gain_ref, *refs):
    text_in, image_in, text_plain, image_plain, text_adjust, image_adjust = refs[:6]
    out_ref, text_heads, image_heads = refs[6:]
    seq_index = lax.axis_index("seq")
    factor = math.log2(math.e) / math.sqrt(HEAD_DIM)
    text_heads[...] = text_in[...]
    image_heads[...] = image_in[...]
    for stream in range(2):
        plain = text_plain if stream == 0 else image_plain
        adjust = text_adjust if stream == 0 else image_adjust
        size = plan.text_dev if stream == 0 else plan.image_dev
        for half in range(CORES):
            place, valid = place_of(plan, plan.groups[-1][0], half, seq_index)
            rows = slice(half * size, (half + 1) * size)

            @pl.when(valid)
            def _():
                write_heads(
                    plan,
                    lambda lanes: plain[rows, lanes] + adjust[rows, lanes],
                    gain_ref,
                    stream,
                    text_heads if stream == 0 else image_heads,
                    pl.ds(pl.multiple_of(place * size, size), size),
                )

    text_total, image_total = plan.seq * plan.text_dev, plan.seq * plan.image_dev
    image_seg = functools.partial(image_seg_of, lengths_ref=lengths_ref, users=plan.users)
    text_cols = lax.broadcasted_iota(jnp.int32, (1, text_total), 1) // TEXT
    image_cols = image_seg(lax.broadcasted_iota(jnp.int32, (1, image_total), 1))
    image_rows = image_seg(lax.broadcasted_iota(jnp.int32, (image_total, 1), 0))
    step = TEXT
    segs = text_total // step
    hits = (image_rows == image_cols, image_rows == text_cols)
    image_bias = [jnp.where(hit, 0.0, -1e30) for hit in hits]
    text_bias = [jnp.where(image_cols == seg, 0.0, -1e30) for seg in range(segs)]
    text_bias = jnp.concatenate(
        [jnp.broadcast_to(one, (step, image_total)) for one in text_bias], axis=0
    )

    def pair(queries, keys):
        return lax.dot_general(queries, keys, NT, preferred_element_type=jnp.float32)

    def softmax(scores):
        tops = [jnp.max(one, axis=1, keepdims=True) for one in scores]
        top = functools.reduce(jnp.maximum, tops)
        weights = [jnp.exp2(one - top) for one in scores]
        total = sum(jnp.sum(one, axis=1, keepdims=True) for one in weights)
        inverse = 1.0 / total
        return [(one * inverse).astype(jnp.bfloat16) for one in weights]

    def mix(probs, values):
        return jnp.dot(probs, values, preferred_element_type=jnp.float32)

    for head in range(plan.heads):
        lanes = slice(head * HEAD_DIM, (head + 1) * HEAD_DIM)
        text_q, text_k, text_v = (text_heads[which, :, lanes] for which in range(3))
        image_q, image_k, image_v = (image_heads[which, :, lanes] for which in range(3))
        spots = [slice(seg * step, (seg + 1) * step) for seg in range(segs)]
        near = jnp.concatenate([pair(text_q[one], text_k[one]) for one in spots], axis=0)
        near, far = softmax([near * factor, pair(text_q, image_k) * factor + text_bias])
        own = jnp.concatenate([mix(near[one], text_v[one]) for one in spots], axis=0)
        result = (own + mix(far, image_v)).astype(jnp.bfloat16)
        for place in range(plan.seq):
            rows = slice(place * plan.text_dev, (place + 1) * plan.text_dev)
            out_ref[place, : plan.text_dev, lanes] = result[rows]
        near, far = softmax(
            [
                pair(image_q, keys) * factor + bias
                for keys, bias in zip((image_k, text_k), image_bias)
            ]
        )
        result = (mix(near, image_v) + mix(far, text_v)).astype(jnp.bfloat16)
        for place in range(plan.seq):
            rows = slice(place * plan.image_dev, (place + 1) * plan.image_dev)
            out_ref[place, plan.text_dev :, lanes] = result[rows]


def attention(plan, lengths, norm_gain, arrays):
    text_total, image_total = plan.seq * plan.text_dev, plan.seq * plan.image_dev
    return pl.pallas_call(
        functools.partial(attend_kernel, plan),
        out_shape=jax.ShapeDtypeStruct((plan.seq, plan.rows, plan.wide), jnp.bfloat16),
        in_specs=[SMEM()] + [VMEM()] * (1 + len(arrays)),
        out_specs=VMEM(),
        scratch_shapes=[
            pltpu.VMEM((3, text_total, plan.wide), jnp.bfloat16),
            pltpu.VMEM((3, image_total, plan.wide), jnp.bfloat16),
        ],
        compiler_params=PARAMS,
        name="attention",
    )(lengths, norm_gain, *arrays)


def place_kernel(plan, pieces, text_out, image_out):
    for place in range(plan.seq):
        lanes = slice(place * plan.wide, (place + 1) * plan.wide)
        text_out[:, lanes] = pieces[place, : plan.text_dev, :]
        image_out[:, lanes] = pieces[place, plan.text_dev :, :]


def placed(plan, pieces):
    sizes = (plan.text_dev, plan.image_dev)
    return pl.pallas_call(
        functools.partial(place_kernel, plan),
        out_shape=tuple(
            jax.ShapeDtypeStruct((n, plan.seq * plan.wide), jnp.bfloat16) for n in sizes
        ),
        in_specs=[VMEM()],
        out_specs=(VMEM(), VMEM()),
        compiler_params=PARAMS,
        name="placed",
    )(pieces)


def steps(
    text_rows,
    image_rows,
    modulation,
    head_weight,
    norm_gain,
    store_down,
    store_up,
    store_row,
    user_adapter,
    image_lengths,
):
    seq, bags = lax.axis_size("seq"), lax.axis_size("bag")
    plan = Plan(
        seq,
        bags,
        text_rows.shape[0],
        image_rows.shape[0],
        image_lengths.shape[1],
        text_rows.shape[1],
        store_up.shape[2],
        store_down.shape[2],
        store_down.shape[0],
        head_weight.shape[2],
    )
    swap = plan.on_cores([(z, z) for z in range(plan.chips)], 1)

    hidden = hidden_rows(plan, image_lengths, text_rows, image_rows, modulation)
    blocks = {("own", 0, 0): hidden, ("own", 0, 1): lax.ppermute(hidden, "seq", swap)}
    passing = [blocks["own", 0, 0], blocks["own", 0, 1]]
    for hop in range(1, plan.chips):
        up = [(2 * z + 1, 2 * z + 3) for z in range(hop - 1, plan.chips - 1)]
        down = [(2 * z, 2 * z - 2) for z in range(1, plan.chips - hop + 1)]
        for half in range(CORES):
            passing[half] = lax.ppermute(passing[half], "seq", up + down)
            other = lax.ppermute(passing[half], "seq", swap)
            if 2 * hop < plan.chips:
                blocks["near", hop, half] = passing[half]
                blocks["far", hop, half] = other
            else:
                blocks["both", hop, half] = (passing[half], other)

    packs = packed_adapters(plan, store_row, user_adapter, store_down, store_up)
    arrived = {}
    for kind, sent in (("down", packs[:bags]), ("up", packs[bags:])):
        arrived[kind] = [sent[0]] + [
            lax.ppermute(sent[hop], "bag", [(b, b ^ hop) for b in range(bags)])
            for hop in range(1, bags)
        ]
    down_shape = (plan.parts, plan.down_rows, plan.cols)
    down_own = jnp.concatenate([one.reshape(down_shape) for one in arrived["down"]], axis=1)
    low, high = plan.half - 1, plan.half
    downs = [down_own] + [
        lax.ppermute(down_own, "seq", plan.on_cores([(low - hop, low), (high + hop, high)]))
        for hop in range(1, plan.half)
    ]

    def blocks_of(slots):
        found = [blocks[kind, hop, half] for kind, hop in slots for half in range(CORES)]
        return [one for pick in found for one in (pick if isinstance(pick, tuple) else (pick,))]

    plains = []
    for group in plan.groups:
        plains.append(project(plan, group, blocks_of(group), head_weight))
    scalars = (image_lengths, store_row, user_adapter)
    before, turned = rank_parts(plan, plan.groups[0], *scalars, downs, blocks_of(plan.groups[0]))
    (ranks,) = rank_parts(
        plan, plan.groups[1], *scalars, [turned, before], blocks_of(plan.groups[1])
    )
    ranks = [jnp.stack([ranks, lax.ppermute(ranks, "seq", swap)])]
    for away in range(1, plan.half + 1):
        pairs = []
        for chip in (low, high):
            pairs += [(2 * chip + 1, 2 * (chip + away) + 1)] * (chip + away < plan.chips)
            pairs += [(2 * chip, 2 * (chip - away))] * (chip >= away)
        ranks.append(lax.ppermute(ranks[0], "seq", pairs))
    ranks += [lax.ppermute(ranks[away], "seq", swap) for away in range(1, plan.half + 1)]

    arrays = early_heads(
        plan,
        plan.groups[:-1],
        *scalars,
        norm_gain,
        ranks,
        arrived["up"],
        [one for pair in plains[:-1] for one in pair],
    )
    outs = attention(
        plan, image_lengths, norm_gain, list(arrays[:2]) + list(plains[-1]) + list(arrays[2:])
    )
    pieces = lax.all_to_all(outs, "seq", split_axis=0, concat_axis=0, tiled=True)
    return placed(plan, pieces)


def solution(mesh):
    in_specs = (
        P(("bag", "seq"), None),
        P(("bag", "seq"), None),
        P("bag", None, None, None),
        P(None, None, "seq"),
        P(),
        P("bag", None, "seq", None),
        P("bag", None, None, "seq"),
        P(),
        P(),
        P("bag", None),
    )
    out_specs = (P(("bag", "seq"), None), P(("bag", "seq"), None))
    return jax.shard_map(steps, mesh=mesh, in_specs=in_specs, out_specs=out_specs, check_vma=False)
```

```python
import functools
import math

import jax
import jax.numpy as jnp
from jax import lax
from jax.experimental import pallas as pl
from jax.experimental.pallas import tpu as pltpu
from jax.sharding import PartitionSpec as P


HEAD_DIM = 128
TEXT = 64
CORES = 2
ROW_STEP = 16


WIDE_GRANT = 59 << 20
VMEM_GRANT = 26 << 20
PARAMS = pltpu.CompilerParams(vmem_limit_bytes=VMEM_GRANT)

SMEM = functools.partial(pl.BlockSpec, memory_space=pltpu.SMEM)
VMEM = functools.partial(pl.BlockSpec, memory_space=pltpu.VMEM)
HBM = functools.partial(pl.BlockSpec, memory_space=pltpu.HBM)
NT = (((1,), (1,)), ((), ()))


def chip_core(seq_index):
    return lax.shift_right_logical(seq_index, CORES // 2), lax.bitwise_and(seq_index, CORES - 1)


def round_up(value, step):
    return -(-value // step) * step


class Plan:
    def __init__(self, seq, bags, text_dev, image_dev, users, width, rank, down_dev, store, cols):
        self.seq, self.bags, self.users, self.rank, self.store = seq, bags, users, rank, store
        self.text_dev, self.image_dev, self.width, self.cols = text_dev, image_dev, width, cols
        self.rows = text_dev + image_dev
        self.chips = seq // CORES
        self.half = self.chips // 2
        self.down_dev = down_dev
        self.down_rows = round_up(2 * down_dev, 16)
        self.parts = width // cols
        self.heads = cols // (3 * HEAD_DIM)
        self.wide = self.heads * HEAD_DIM
        self.lanes = round_up(self.rows, 128)
        self.groups = [[("own", 0)]]
        for hop in range(1, self.chips):
            if 2 * hop < self.chips:
                self.groups[0] += [("near", hop), ("far", hop)]
            else:
                self.groups.append([("both", hop)])

    def on_cores(self, pairs, cross=0):
        return [
            (CORES * a + c, CORES * b + (c ^ cross)) for a, b in pairs for c in range(CORES)
        ]


def place_of(plan, slot, half, seq_index):
    chip, core = chip_core(seq_index)
    kind, hop = slot
    if kind == "own":
        source, lead = chip, core
    elif kind == "near":
        source, lead = jnp.where(core == 1, chip - hop, chip + hop), core
    elif kind == "far":
        source, lead = jnp.where(core == 1, chip + hop, chip - hop), 1 - core
    else:
        low = chip >= hop
        source, lead = jnp.where(low, chip - hop, chip + hop), jnp.where(low, 1, 0)
    valid = (source >= 0) & (source < plan.chips)
    source = jnp.clip(source, 0, plan.chips - 1)
    return source * CORES + (lead if half == 0 else 1 - lead), valid


def refs_per_half(slots):
    return CORES if slots[0][0] == "both" else 1


def is_passed(plan, slot, seq_index):
    chip, core = chip_core(seq_index)
    return jnp.where(core == 1, chip >= slot[1], chip + slot[1] < plan.chips)


def user_keys(plan, store_row_ref, adapter_ref):
    bag, keys = lax.axis_index("bag"), []
    for user in range(plan.users):
        row, owner = store_row_ref[adapter_ref[bag, user]], jnp.int32(0)
        for other in range(1, plan.bags):
            owner = owner + (row >= other * plan.store).astype(jnp.int32)
        keys.append(lax.bitwise_xor(owner, bag))
    return keys


def image_seg_of(position, lengths_ref, users):
    seg = jnp.zeros_like(position)
    end = jnp.int32(0)
    for user in range(users):
        for _ in range(2):
            end = end + lengths_ref[0, user]
            seg = seg + (position >= end).astype(jnp.int32)
    return seg


def hidden_kernel(plan, lengths_ref, text_ref, image_ref, mod_ref, out_ref):
    seq_index = lax.axis_index("seq")
    segs = mod_ref.shape[0]

    def normed(rows):
        values = rows.astype(jnp.float32)
        centre = values - jnp.mean(values, axis=-1, keepdims=True)
        spread = jnp.mean(centre * centre, axis=-1, keepdims=True)
        return centre * lax.rsqrt(spread + 1e-06)

    def image_step(step, _):
        rows = pl.ds(pl.multiple_of(step * ROW_STEP, ROW_STEP), ROW_STEP)
        place = seq_index * plan.image_dev + step * ROW_STEP
        position = place + lax.broadcasted_iota(jnp.int32, (ROW_STEP, 1), 0)
        seg = image_seg_of(position, lengths_ref, plan.users)
        base = normed(image_ref[rows, :])
        shift = jnp.zeros_like(base)
        scale = jnp.zeros_like(base)
        for one in range(segs):
            hit = seg == one
            shift = jnp.where(hit, mod_ref[one, 1, 0:1, :], shift)
            scale = jnp.where(hit, mod_ref[one, 1, 1:2, :], scale)
        target = pl.ds(pl.multiple_of(plan.text_dev + step * ROW_STEP, ROW_STEP), ROW_STEP)
        out_ref[target, :] = ((1.0 + scale) * base + shift).astype(jnp.bfloat16)
        return 0

    lax.fori_loop(0, plan.image_dev // ROW_STEP, image_step, 0, unroll=True)

    def text_step(step, _):
        rows = pl.ds(pl.multiple_of(step * ROW_STEP, ROW_STEP), ROW_STEP)
        seg = (seq_index * plan.text_dev + step * ROW_STEP) // TEXT
        shift = mod_ref[seg, 0, 0:1, :]
        scale = mod_ref[seg, 0, 1:2, :]
        out_ref[rows, :] = ((1.0 + scale) * normed(text_ref[rows, :]) + shift).astype(jnp.bfloat16)
        return 0

    lax.fori_loop(0, plan.text_dev // ROW_STEP, text_step, 0, unroll=True)


def hidden_rows(plan, lengths, text_rows, image_rows, modulation):
    return pl.pallas_call(
        functools.partial(hidden_kernel, plan),
        out_shape=jax.ShapeDtypeStruct((plan.rows, plan.width), jnp.bfloat16),
        in_specs=[SMEM(), VMEM(), VMEM(), VMEM()],
        out_specs=VMEM(),
        compiler_params=pltpu.CompilerParams(vmem_limit_bytes=WIDE_GRANT),
        name="hidden_rows",
    )(lengths, text_rows, image_rows, modulation)


def pack_kernel(plan, store_row_ref, adapter_ref, down_hbm, up_hbm, *rest):
    outs, ups, rest = rest[: plan.bags], rest[plan.bags : 2 * plan.bags], rest[2 * plan.bags :]
    down, up, down_sem, up_sem = rest
    bag = lax.axis_index("bag")
    copies = []
    for hop in range(plan.bags):
        target = lax.bitwise_xor(bag, hop)
        place = jnp.int32(0)
        for user in range(plan.users):
            row = store_row_ref[adapter_ref[target, user]]
            row = row - bag * plan.store
            place = jnp.where((row >= 0) & (row < plan.store), row, place)
        one = pltpu.make_async_copy(down_hbm.at[place], down.at[hop], down_sem.at[hop])
        two = pltpu.make_async_copy(up_hbm.at[place], up.at[hop], up_sem.at[hop])
        one.start()
        two.start()
        copies.append((one, two))
    pad = plan.down_rows - 2 * plan.down_dev
    for hop in range(plan.bags):
        copies[hop][0].wait()
        for part in range(plan.parts):
            lanes = slice(part * plan.cols, (part + 1) * plan.cols)
            rows = [down[hop, t, :, lanes].astype(jnp.float32) for t in range(2)]
            if pad:
                rows.append(jnp.zeros((pad, plan.cols), jnp.float32))
            spot = slice(part * plan.down_rows, (part + 1) * plan.down_rows)
            outs[hop][spot, :] = jnp.concatenate(rows, axis=0).astype(jnp.bfloat16)
        copies[hop][1].wait()
        for t in range(2):
            ups[hop][t * plan.rank : (t + 1) * plan.rank, :] = up[hop, t]


def packed_adapters(plan, store_row, user_adapter, store_down, store_up):
    sizes = (plan.parts * plan.down_rows, 2 * plan.rank)
    return pl.pallas_call(
        functools.partial(pack_kernel, plan),
        out_shape=[
            jax.ShapeDtypeStruct((rows, plan.cols), jnp.bfloat16)
            for rows in sizes
            for _ in range(plan.bags)
        ],
        in_specs=[SMEM()] * 2 + [HBM(), HBM()],
        out_specs=[VMEM()] * (2 * plan.bags),
        scratch_shapes=[
            pltpu.VMEM((plan.bags,) + store_down.shape[1:], jnp.bfloat16),
            pltpu.VMEM((plan.bags,) + store_up.shape[1:], jnp.bfloat16),
            pltpu.SemaphoreType.DMA((plan.bags,)),
            pltpu.SemaphoreType.DMA((plan.bags,)),
        ],
        compiler_params=pltpu.CompilerParams(vmem_limit_bytes=52 << 20),
        name="packed_adapters",
    )(store_row, user_adapter, store_down, store_up)


def project_kernel(plan, slots, *refs):
    blocks, (weight_ref, text_out, image_out, texts, images) = refs[:-5], refs[-5:]
    text_dev, image_dev, each = plan.text_dev, plan.image_dev, refs_per_half(slots)

    def take(at, block):
        texts[at * text_dev : (at + 1) * text_dev, :] = block[:text_dev, :]
        images[at * image_dev : (at + 1) * image_dev, :] = block[text_dev:, :]

    if each == 1:
        for at, block in enumerate(blocks):
            take(at, block)
    else:
        passed = is_passed(plan, slots[0], lax.axis_index("seq"))
        for choice in range(2):

            @pl.when(passed if choice == 0 else jnp.logical_not(passed))
            def _():
                for at in range(CORES):
                    take(at, blocks[2 * at + choice])

    def multiply():
        text_out[...] = jnp.dot(texts[...], weight_ref[0], preferred_element_type=jnp.float32)
        image_out[...] = jnp.dot(images[...], weight_ref[1], preferred_element_type=jnp.float32)

    if each == 1:
        multiply()
    else:
        _, valid = place_of(plan, slots[0], 0, lax.axis_index("seq"))
        pl.when(valid)(multiply)


def project(plan, slots, blocks, head_weight):
    count = CORES * len(slots)
    sizes = (count * plan.text_dev, count * plan.image_dev)
    return pl.pallas_call(
        functools.partial(project_kernel, plan, slots),
        out_shape=tuple(jax.ShapeDtypeStruct((size, plan.cols), jnp.float32) for size in sizes),
        in_specs=[VMEM()] * (len(blocks) + 1),
        out_specs=(VMEM(), VMEM()),
        scratch_shapes=[pltpu.VMEM((size, plan.width), jnp.bfloat16) for size in sizes],
        compiler_params=PARAMS,
        cost_estimate=pl.CostEstimate(
            flops=2 * sum(sizes) * plan.width * plan.cols,
            bytes_accessed=2 * sum(sizes) * plan.width,
            transcendentals=0,
        ),
    )(*blocks, head_weight)


def lane_keys(plan, lengths_ref, keys, place):
    lane = lax.broadcasted_iota(jnp.int32, (1, plan.lanes), 1)
    is_text = lane < plan.text_dev
    text_seg = (place * plan.text_dev + lane) // TEXT
    image_at = place * plan.image_dev + lane - plan.text_dev
    seg = jnp.where(is_text, text_seg, image_seg_of(image_at, lengths_ref, plan.users))
    key = jnp.zeros_like(lane)
    for user in range(plan.users):
        key = jnp.where(seg // 2 == user, keys[user], key)
    return key, is_text


def rank_kernel(plan, slots, lengths_ref, store_row_ref, adapter_ref, *refs):
    halves = CORES * len(slots)
    each = refs_per_half(slots)
    first = slots[0][0] == "own"
    given = plan.half if first else 2
    downs, refs = refs[:given], refs[given:]
    blocks, refs = refs[: each * halves], refs[each * halves :]
    if first:
        out_ref, turned, stacked = refs
    else:
        (out_ref,), (turned, before) = refs, downs
        out_ref[...] = before[...]
    seq_index = lax.axis_index("seq")
    chip, _ = chip_core(seq_index)
    passed = is_passed(plan, slots[0], seq_index)
    keys = user_keys(plan, store_row_ref, adapter_ref)
    tall = plan.bags * plan.down_rows
    for part in range(plan.parts if first else 0):
        lanes = slice(part * plan.cols, (part + 1) * plan.cols)
        for index, down_ref in enumerate(downs):
            stacked[index * tall : (index + 1) * tall, :] = down_ref[part].astype(jnp.float32)
        turned[lanes, :] = jnp.transpose(stacked[...]).astype(jnp.bfloat16)
    for at in range(halves):
        place, valid = place_of(plan, slots[at // CORES], at % CORES, seq_index)
        block = blocks[each * at][...]
        if each > 1:
            block = jnp.where(passed, block, blocks[each * at + 1][...])
        found = jnp.dot(block, turned[...], preferred_element_type=jnp.float32)
        found = jnp.transpose(found)
        if plan.rows < plan.lanes:
            pad = jnp.zeros((found.shape[0], plan.lanes - plan.rows), jnp.float32)
            found = jnp.concatenate([found, pad], axis=1)
        key, is_text = lane_keys(plan, lengths_ref, keys, place)
        for index in range(plan.half):
            total = jnp.zeros((plan.down_dev, plan.lanes), jnp.float32)
            for hop in range(plan.bags):
                top = index * tall + hop * plan.down_rows
                text_part = found[top : top + plan.down_dev]
                image_part = found[top + plan.down_dev : top + 2 * plan.down_dev]
                total = total + jnp.where(
                    key == hop, jnp.where(is_text, text_part, image_part), 0.0
                )
            spot = jnp.where(chip < plan.half, plan.half - 1 - index, index)

            @pl.when(valid)
            def _():
                out_ref[spot, place] = total.astype(jnp.bfloat16)


def rank_parts(plan, slots, scalars, downs, blocks):
    first = slots[0][0] == "own"
    tall = plan.half * plan.bags * plan.down_rows
    rows = plan.rows * CORES * len(slots)
    out_shape = [
        jax.ShapeDtypeStruct((plan.half, plan.seq, plan.down_dev, plan.lanes), jnp.bfloat16)
    ]
    if first:
        out_shape.append(jax.ShapeDtypeStruct((plan.width, tall), jnp.bfloat16))
    return pl.pallas_call(
        functools.partial(rank_kernel, plan, slots),
        out_shape=out_shape,
        in_specs=[SMEM()] * 3 + [VMEM()] * (len(downs) + len(blocks)),
        out_specs=[VMEM()] * len(out_shape),
        scratch_shapes=[pltpu.VMEM((tall, plan.cols), jnp.float32)] if first else [],
        compiler_params=PARAMS,
        cost_estimate=pl.CostEstimate(
            flops=(64 if first else 1) * rows * plan.width * tall,
            bytes_accessed=2 * rows * plan.width,
            transcendentals=0,
        ),
        name="rank_parts",
    )(*scalars, *downs, *blocks)


def head_normed(values, gain_row):
    spread = jnp.mean(values * values, axis=-1, keepdims=True)
    return (values * lax.rsqrt(spread + 1e-06) * gain_row).astype(jnp.bfloat16)


def write_heads(plan, mixed_of, gain_ref, stream, out_ref, rows):
    for head in range(plan.heads):
        for which in range(3):
            first = (3 * head + which) * HEAD_DIM
            mixed = mixed_of(slice(first, first + HEAD_DIM))
            if which < 2:
                mixed = head_normed(mixed, gain_ref[stream, which : which + 1, :])
            lanes = slice(head * HEAD_DIM, (head + 1) * HEAD_DIM)
            out_ref[which, rows, lanes] = mixed.astype(jnp.bfloat16)


def early_kernel(plan, groups, lengths_ref, store_row_ref, adapter_ref, gain_ref, *refs):
    ranks, refs = refs[: 2 * plan.half + 1], refs[2 * plan.half + 1 :]
    packs, refs = refs[: plan.bags], refs[plan.bags :]
    plains, refs = refs[: 2 * len(groups)], refs[2 * len(groups) :]
    text_heads, image_heads, text_last, image_last, ranks_ref, spread, text_side, image_side, ups = refs[:9]
    sides, adjusts = (text_side, image_side), refs[9:]
    seq_index = lax.axis_index("seq")
    chip, core = chip_core(seq_index)
    leads = []
    for side, middle in enumerate((plan.half - 1, plan.half)):
        away = jnp.abs(chip - middle)
        sender = jnp.where(away == 0, core, (chip > middle).astype(jnp.int32))
        leads.append(sender)
        for at, source in enumerate(ranks):
            hop = at if at <= plan.half else at - plan.half
            here = (away == hop) & ((sender == core) if at <= plan.half else (sender != core))

            @pl.when(here)
            def _():
                ranks_ref[side] = source[...]

    keys = user_keys(plan, store_row_ref, adapter_ref)
    for place in range(plan.seq):
        key, _ = lane_keys(plan, lengths_ref, keys, place)
        for side in range(2):
            for lead in range(CORES):
                for index in range(plan.half):
                    rows = ranks_ref[
                        side, lax.bitwise_xor(leads[side], lead), index, place
                    ].astype(jnp.float32)
                    first = ((side * plan.half + index) * CORES + lead) * plan.down_dev
                    for hop in range(plan.bags):
                        top = hop * plan.rank + first
                        spread[place, top : top + plan.down_dev, :] = jnp.where(
                            key == hop, rows, 0.0
                        )
        turned = jnp.transpose(spread[place]).astype(jnp.bfloat16)
        for stream, size, skip in ((0, plan.text_dev, 0), (1, plan.image_dev, plan.text_dev)):
            sides[stream][place * size : (place + 1) * size, :] = turned[skip : skip + size, :]
    for stream in range(2):
        for hop in range(plan.bags):
            ups[hop * plan.rank : (hop + 1) * plan.rank, :] = packs[hop][
                stream * plan.rank : (stream + 1) * plan.rank, :
            ]
        adjusts[stream][...] = jnp.dot(
            sides[stream][...], ups[...], preferred_element_type=jnp.float32
        )

    sizes = (plan.text_dev, plan.image_dev)
    outs = (text_heads, image_heads)

    def rows_of(place, size):
        return pl.ds(pl.multiple_of(place * size, size), size)

    for group_at, group in enumerate(groups):
        for slot_at, slot in enumerate(group):
            _, valid = place_of(plan, slot, 0, seq_index)

            @pl.when(valid)
            def _():
                for half in range(CORES):
                    place, _ = place_of(plan, slot, half, seq_index)
                    at = slot_at * CORES + half
                    for stream, size in enumerate(sizes):
                        plain = plains[2 * group_at + stream]
                        spot = rows_of(place, size)
                        write_heads(
                            plan,
                            lambda lanes: plain[at * size : (at + 1) * size, lanes]
                            + adjusts[stream][spot, lanes],
                            gain_ref,
                            stream,
                            outs[stream],
                            spot,
                        )

    for half in range(CORES):
        place, _ = place_of(plan, plan.groups[-1][0], half, seq_index)
        for stream, size in enumerate(sizes):
            last_ref = (text_last, image_last)[stream]
            last_ref[half * size : (half + 1) * size, :] = adjusts[stream][
                rows_of(place, size), :
            ]


def early_heads(plan, groups, scalars, norm_gain, ranks, packs, plains):
    total = (plan.seq * plan.text_dev, plan.seq * plan.image_dev)
    last = (CORES * plan.text_dev, CORES * plan.image_dev)
    scratch = 4 * plan.seq * plan.lanes * (plan.bags * plan.rank + plan.cols)
    return pl.pallas_call(
        functools.partial(early_kernel, plan, groups),
        out_shape=tuple(jax.ShapeDtypeStruct((3, n, plan.wide), jnp.bfloat16) for n in total)
        + tuple(jax.ShapeDtypeStruct((n, plan.cols), jnp.float32) for n in last),
        in_specs=[SMEM()] * 3 + [VMEM()] * (1 + len(ranks) + plan.bags + len(plains)),
        out_specs=(VMEM(),) * 4,
        scratch_shapes=[
            pltpu.VMEM((2,) + ranks[0].shape, jnp.bfloat16),
            pltpu.VMEM((plan.seq, plan.bags * plan.rank, plan.lanes), jnp.float32),
            pltpu.VMEM((total[0], plan.bags * plan.rank), jnp.bfloat16),
            pltpu.VMEM((total[1], plan.bags * plan.rank), jnp.bfloat16),
            pltpu.VMEM((plan.bags * plan.rank, plan.cols), jnp.bfloat16),
            pltpu.VMEM((total[0], plan.cols), jnp.float32),
            pltpu.VMEM((total[1], plan.cols), jnp.float32),
        ],
        compiler_params=pltpu.CompilerParams(vmem_limit_bytes=max(VMEM_GRANT, 2 * scratch)),
        cost_estimate=pl.CostEstimate(
            flops=4 * plan.seq * plan.lanes * plan.bags * plan.rank * plan.cols,
            bytes_accessed=8 * sum(total) * plan.cols,
            transcendentals=0,
        ),
        name="early_heads",
    )(*scalars, norm_gain, *ranks, *packs, *plains)


def attend_kernel(plan, lengths_ref, gain_ref, *refs):
    text_in, image_in, text_plain, image_plain, text_adjust, image_adjust = refs[:6]
    out_ref, text_heads, image_heads = refs[6:]
    seq_index = lax.axis_index("seq")
    factor = math.log2(math.e) / math.sqrt(HEAD_DIM)
    text_heads[...] = text_in[...]
    image_heads[...] = image_in[...]
    last = plan.groups[-1][0]
    _, valid = place_of(plan, last, 0, seq_index)

    @pl.when(valid)
    def _():
        for half in range(CORES):
            place, _ = place_of(plan, last, half, seq_index)
            for stream, plain, adjust, out, size in (
                (0, text_plain, text_adjust, text_heads, plan.text_dev),
                (1, image_plain, image_adjust, image_heads, plan.image_dev),
            ):
                rows = slice(half * size, (half + 1) * size)
                write_heads(
                    plan,
                    lambda lanes: plain[rows, lanes] + adjust[rows, lanes],
                    gain_ref,
                    stream,
                    out,
                    pl.ds(pl.multiple_of(place * size, size), size),
                )

    text_total, image_total = plan.seq * plan.text_dev, plan.seq * plan.image_dev
    image_seg = functools.partial(image_seg_of, lengths_ref=lengths_ref, users=plan.users)
    text_cols = lax.broadcasted_iota(jnp.int32, (1, text_total), 1) // TEXT
    image_cols = image_seg(lax.broadcasted_iota(jnp.int32, (1, image_total), 1))
    image_rows = image_seg(lax.broadcasted_iota(jnp.int32, (image_total, 1), 0))
    step = TEXT
    segs = text_total // step
    hits = (image_rows == image_cols, image_rows == text_cols)
    image_bias = [jnp.where(hit, 0.0, -1e30) for hit in hits]
    text_bias = [jnp.where(image_cols == seg, 0.0, -1e30) for seg in range(segs)]
    text_bias = jnp.concatenate(
        [jnp.broadcast_to(one, (step, image_total)) for one in text_bias], axis=0
    )

    def pair(queries, keys):
        return lax.dot_general(queries, keys, NT, preferred_element_type=jnp.float32)

    def softmax(scores):
        tops = [jnp.max(one, axis=1, keepdims=True) for one in scores]
        top = functools.reduce(jnp.maximum, tops)
        weights = [jnp.exp2(one - top) for one in scores]
        total = sum(jnp.sum(one, axis=1, keepdims=True) for one in weights)
        inverse = 1.0 / total
        return [(one * inverse).astype(jnp.bfloat16) for one in weights]

    def mix(probs, values):
        return jnp.dot(probs, values, preferred_element_type=jnp.float32)

    for head in range(plan.heads):
        lanes = slice(head * HEAD_DIM, (head + 1) * HEAD_DIM)
        text_q, text_k, text_v = (text_heads[which, :, lanes] for which in range(3))
        image_q, image_k, image_v = (image_heads[which, :, lanes] for which in range(3))
        spots = [slice(seg * step, (seg + 1) * step) for seg in range(segs)]
        near = jnp.concatenate([pair(text_q[one], text_k[one]) for one in spots], axis=0)
        near, far = softmax([near * factor, pair(text_q, image_k) * factor + text_bias])
        own = jnp.concatenate([mix(near[one], text_v[one]) for one in spots], axis=0)
        result = (own + mix(far, image_v)).astype(jnp.bfloat16)
        for place in range(plan.seq):
            rows = slice(place * plan.text_dev, (place + 1) * plan.text_dev)
            out_ref[place, : plan.text_dev, lanes] = result[rows]
        near, far = softmax(
            [
                pair(image_q, keys) * factor + bias
                for keys, bias in zip((image_k, text_k), image_bias)
            ]
        )
        result = (mix(near, image_v) + mix(far, text_v)).astype(jnp.bfloat16)
        for place in range(plan.seq):
            rows = slice(place * plan.image_dev, (place + 1) * plan.image_dev)
            out_ref[place, plan.text_dev :, lanes] = result[rows]


def attention(plan, lengths, norm_gain, arrays):
    text_total, image_total = plan.seq * plan.text_dev, plan.seq * plan.image_dev
    return pl.pallas_call(
        functools.partial(attend_kernel, plan),
        out_shape=jax.ShapeDtypeStruct((plan.seq, plan.rows, plan.wide), jnp.bfloat16),
        in_specs=[SMEM()] + [VMEM()] * (1 + len(arrays)),
        out_specs=VMEM(),
        scratch_shapes=[
            pltpu.VMEM((3, text_total, plan.wide), jnp.bfloat16),
            pltpu.VMEM((3, image_total, plan.wide), jnp.bfloat16),
        ],
        compiler_params=PARAMS,
        name="attention",
    )(lengths, norm_gain, *arrays)


def place_kernel(plan, pieces, text_out, image_out):
    for place in range(plan.seq):
        lanes = slice(place * plan.wide, (place + 1) * plan.wide)
        text_out[:, lanes] = pieces[place, : plan.text_dev, :]
        image_out[:, lanes] = pieces[place, plan.text_dev :, :]


def placed(plan, pieces):
    sizes = (plan.text_dev, plan.image_dev)
    return pl.pallas_call(
        functools.partial(place_kernel, plan),
        out_shape=tuple(
            jax.ShapeDtypeStruct((n, plan.seq * plan.wide), jnp.bfloat16) for n in sizes
        ),
        in_specs=[VMEM()],
        out_specs=(VMEM(), VMEM()),
        compiler_params=PARAMS,
        name="placed",
    )(pieces)


def steps(
    text_rows,
    image_rows,
    modulation,
    head_weight,
    norm_gain,
    store_down,
    store_up,
    store_row,
    user_adapter,
    image_lengths,
):
    seq, bags = lax.axis_size("seq"), lax.axis_size("bag")
    plan = Plan(
        seq,
        bags,
        text_rows.shape[0],
        image_rows.shape[0],
        image_lengths.shape[1],
        text_rows.shape[1],
        store_up.shape[2],
        store_down.shape[2],
        store_down.shape[0],
        head_weight.shape[2],
    )
    swap = plan.on_cores([(z, z) for z in range(plan.chips)], 1)

    hidden = hidden_rows(plan, image_lengths, text_rows, image_rows, modulation)
    blocks = {("own", 0, 0): hidden, ("own", 0, 1): lax.ppermute(hidden, "seq", swap)}
    passing = [blocks["own", 0, 0], blocks["own", 0, 1]]
    for hop in range(1, plan.chips):
        up = [(2 * z + 1, 2 * z + 3) for z in range(hop - 1, plan.chips - 1)]
        down = [(2 * z, 2 * z - 2) for z in range(1, plan.chips - hop + 1)]
        for half in range(CORES):
            passing[half] = lax.ppermute(passing[half], "seq", up + down)
            other = lax.ppermute(passing[half], "seq", swap)
            if 2 * hop < plan.chips:
                blocks["near", hop, half] = passing[half]
                blocks["far", hop, half] = other
            else:
                blocks["both", hop, half] = (passing[half], other)

    packs = packed_adapters(plan, store_row, user_adapter, store_down, store_up)
    arrived = {}
    for kind, sent in (("down", packs[:bags]), ("up", packs[bags:])):
        arrived[kind] = [sent[0]] + [
            lax.ppermute(sent[hop], "bag", [(b, b ^ hop) for b in range(bags)])
            for hop in range(1, bags)
        ]
    down_shape = (plan.parts, plan.down_rows, plan.cols)
    down_own = jnp.concatenate([one.reshape(down_shape) for one in arrived["down"]], axis=1)
    low, high = plan.half - 1, plan.half
    downs = [down_own] + [
        lax.ppermute(down_own, "seq", plan.on_cores([(low - hop, low), (high + hop, high)]))
        for hop in range(1, plan.half)
    ]

    def blocks_of(slots):
        found = [blocks[kind, hop, half] for kind, hop in slots for half in range(CORES)]
        return [one for pick in found for one in (pick if isinstance(pick, tuple) else (pick,))]

    plains = []
    for group in plan.groups:
        plains.append(project(plan, group, blocks_of(group), head_weight))
    scalars = (image_lengths, store_row, user_adapter)
    before, turned = rank_parts(
        plan, plan.groups[0], scalars, downs, blocks_of(plan.groups[0])
    )
    (ranks,) = rank_parts(
        plan, plan.groups[1], scalars, [turned, before], blocks_of(plan.groups[1])
    )
    ranks = [jnp.stack([ranks, lax.ppermute(ranks, "seq", swap)])]
    for away in range(1, plan.half + 1):
        pairs = []
        for chip in (low, high):
            pairs += [(2 * chip + 1, 2 * (chip + away) + 1)] * (chip + away < plan.chips)
            pairs += [(2 * chip, 2 * (chip - away))] * (chip >= away)
        ranks.append(lax.ppermute(ranks[0], "seq", pairs))
    ranks += [lax.ppermute(ranks[away], "seq", swap) for away in range(1, plan.half + 1)]

    arrays = early_heads(
        plan,
        plan.groups[:-1],
        scalars, norm_gain,
        ranks,
        arrived["up"],
        [one for pair in plains[:-1] for one in pair],
    )
    outs = attention(
        plan, image_lengths, norm_gain, list(arrays[:2]) + list(plains[-1]) + list(arrays[2:])
    )
    pieces = lax.all_to_all(outs, "seq", split_axis=0, concat_axis=0, tiled=True)
    return placed(plan, pieces)


def solution(mesh):
    in_specs = (
        P(("bag", "seq"), None),
        P(("bag", "seq"), None),
        P("bag", None, None, None),
        P(None, None, "seq"),
        P(),
        P("bag", None, "seq", None),
        P("bag", None, None, "seq"),
        P(),
        P(),
        P("bag", None),
    )
    out_specs = (P(("bag", "seq"), None), P(("bag", "seq"), None))
    return jax.shard_map(steps, mesh=mesh, in_specs=in_specs, out_specs=out_specs, check_vma=False)
```
